32 devices in a mesh: loop: 16 (over z, y, x), rep: 2 (over core).
Axes of the slice: x: 2, y: 2, z: 4, core: 2. Of those that a mesh axis runs over, the one named last changes fastest.
Arguments:
- node_features: bfloat16 [4096, 256], P(('loop', 'rep')), may hold values from -6 to 6
- weight: bfloat16 [256, 256], replicated, may hold values from -0.375 to 0.375
- bias_vector: float32 [256], replicated, may hold values from -3 to 3
- tile_values: bfloat16 [16, 2, 16, 2, 128, 128], P('loop', 'rep'), may hold values from 0 to 0.029907227
- tile_place: int32 [16, 2, 16, 2], P('loop', 'rep'), may hold values from 0 to 1
- tile_count: int32 [16, 2, 16], P('loop', 'rep'), may hold values from 0 to 2, as said below
- cotangent: bfloat16 [4096, 256], P(('loop', 'rep')), may hold values from -6 to 6
Outputs:
- output: bfloat16 [4096, 256], P(('loop', 'rep'))
- grad_features: bfloat16 [4096, 256], P(('loop', 'rep'))
- grad_weight: float32 [256, 256], replicated
- grad_bias: float32 [256], replicated
The draws below stay inside these ranges and needn't reach their ends.
Inputs may be any that keep to these rules, and one draw needn't show every extreme that they name: Slot s of list [i, r, p] is live exactly when s < tile_count[i, r, p]; lists of some devices are far fuller than those of others.
All inputs are finite; a program needn't handle non-finite values.
Results may differ from the reference program's by a relative error of at most 0.0053.
Values may be sent and summed in bfloat16 or wider, within the bound.
No kernel may reach another device: no remote copies, remote signals or barrier semaphores. Data moves between devices by JAX's collectives and lax.ppermute only.
A program may use at most 64 MiB of HBM per device.

```python
import jax
import jax.numpy as jnp
from jax import lax

F = 256
TILE = 128
TPS = 2
RB = 1
REPS = 2
PARTNERS = 16
PANEL_TILES = 2
NODES = 4096


def draw_tile_count(key, part):
    level_key, count_key, kept_key = jax.random.split(key, 3)
    busy_level = jax.random.randint(level_key, (PARTNERS, REPS, 1), 1, 5)
    raw_count = jax.random.randint(count_key, (PARTNERS, REPS, PARTNERS), 0, TPS + 1)
    kept_slots = jax.random.randint(kept_key, (PARTNERS, REPS, PARTNERS), 0, 4) < busy_level
    return jnp.where(kept_slots, raw_count, 0).astype(jnp.int32)


def place_ends(drawn, stream_key, least, high):
    index_at = [jax.random.randint(jax.random.fold_in(stream_key, axis), (), 0, length) for axis, length in enumerate(drawn.shape)]
    widest = drawn.shape.index(max(drawn.shape))
    next_to = index_at[:widest] + [(index_at[widest] + 1) % drawn.shape[widest]] + index_at[widest + 1:]
    return drawn.at[tuple(index_at)].set(least).at[tuple(next_to)].set(high)


def block_levels(rng, dims, cuts, smallest, high):
    factor_of = 1.0
    for position, blocks in cuts:
        draws = jax.random.uniform(jax.random.fold_in(jax.random.fold_in(rng, 6), position), (blocks,), jnp.float32, smallest / len(cuts), high / len(cuts))
        factor_of = factor_of * jnp.repeat(jnp.exp(draws), dims[position] // blocks).reshape((-1,) + (1,) * (len(dims) - 1 - position))
    return factor_of


def centred(key, dims, spread, limit, shards=(), held_as=jnp.bfloat16):
    result = spread * jax.random.normal(key, dims, jnp.float32)
    if shards:
        result = result * block_levels(key, dims, shards, -0.22, 0.18)
    return jnp.clip(result, -limit, limit).astype(held_as)


def setup_inputs(seed: int = 0) -> dict:
    keys = jax.random.split(jax.random.key(seed), 8)
    node_features = centred(keys[0], (NODES, F), 1.0, 6.0, ((0, 32),))
    weight = centred(keys[1], (F, F), F ** -0.5, 0.375)
    bias_vector = centred(keys[2], (F,), 0.5, 3.0, (), jnp.float32)
    tile_values = jnp.clip(0.029907227 * jax.random.uniform(keys[3], (PARTNERS, REPS, PARTNERS, TPS, TILE, TILE), jnp.float32) ** block_levels(keys[3], (PARTNERS, REPS, PARTNERS, TPS, TILE, TILE), ((0, 16), (1, 2)), -0.2, 0.2), 0.0, 0.029907227).astype(jnp.bfloat16)
    tile_place = place_ends(jax.random.randint(keys[4], (PARTNERS, REPS, PARTNERS, TPS), 0, PANEL_TILES * RB), jax.random.fold_in(keys[4], 1), 0, (PANEL_TILES * RB) - 1).astype(jnp.int32)
    tile_count = draw_tile_count(jax.random.fold_in(keys[7], 71), 0)
    cotangent = centred(keys[6], (NODES, F), 1.0, 6.0, ((0, 32),))
    return dict(node_features=node_features, weight=weight, bias_vector=bias_vector, tile_values=tile_values, tile_place=tile_place, tile_count=tile_count, cotangent=cotangent)


def elu_parts(preact):
    negative = jnp.minimum(preact, 0.0)
    value = jnp.where(preact > 0, preact, jnp.expm1(negative))
    slope = jnp.where(preact > 0, 1.0, jnp.exp(negative))
    return value, slope


def reference(node_features, weight, bias_vector, tile_values, tile_place, tile_count, cotangent):
    projected = jnp.dot(node_features, weight, preferred_element_type=jnp.float32).astype(jnp.bfloat16)
    proj_blocks = projected.reshape(PARTNERS, REPS, RB, TILE, F)
    slot_index = jnp.arange(TPS, dtype=jnp.int32)
    live_all = (slot_index[None, None, None, :] < tile_count[..., None]).astype(jnp.float32)
    row_tiles = (tile_place // RB).astype(jnp.int32)
    col_tiles = (tile_place % RB).astype(jnp.int32)
    partner_index = jnp.arange(PARTNERS, dtype=jnp.int32)[None, :, None]
    rep_index = jnp.arange(REPS, dtype=jnp.int32)[:, None, None]

    def panel(loop_pos):
        tiles = tile_values[loop_pos].astype(jnp.float32)
        right_rows = proj_blocks[partner_index, rep_index, col_tiles[loop_pos]].astype(jnp.float32)
        product = jnp.einsum("rpsab,rpsbf->rpsaf", tiles, right_rows)
        product = product * live_all[loop_pos][..., None, None]
        summed = jax.ops.segment_sum(product.reshape(-1, TILE, F), row_tiles[loop_pos].reshape(-1), num_segments=PANEL_TILES)
        return summed.reshape(PANEL_TILES * TILE, F)

    preact = lax.map(panel, jnp.arange(PARTNERS, dtype=jnp.int32)).reshape(NODES, F)
    preact = preact + bias_vector[None, :]
    value, slope = elu_parts(preact)
    output = value.astype(jnp.bfloat16)
    grad_pre = (cotangent.astype(jnp.float32) * slope).astype(jnp.bfloat16)
    grad_panels = grad_pre.reshape(PARTNERS, PANEL_TILES, TILE, F)

    def backward_panel(loop_pos, adjoint):
        tiles = tile_values[loop_pos].astype(jnp.float32)
        left_rows = grad_panels[loop_pos][row_tiles[loop_pos]].astype(jnp.float32)
        product = jnp.einsum("rpsab,rpsaf->rpsbf", tiles, left_rows)
        product = product * live_all[loop_pos][..., None, None]
        targets = ((partner_index * REPS + rep_index) * RB + col_tiles[loop_pos]).astype(jnp.int32)
        summed = jax.ops.segment_sum(product.reshape(-1, TILE, F), targets.reshape(-1), num_segments=PARTNERS * REPS * RB)
        return adjoint + summed

    adjoint = lax.fori_loop(0, PARTNERS, backward_panel, jnp.zeros((PARTNERS * REPS * RB, TILE, F), jnp.float32))
    adjoint_low = adjoint.reshape(NODES, F).astype(jnp.bfloat16)
    grad_features = jnp.dot(adjoint_low, weight.T, preferred_element_type=jnp.float32).astype(jnp.bfloat16)
    scale_factor = float(NODES) ** -0.5
    grad_weight = jnp.dot(node_features.T, adjoint_low, preferred_element_type=jnp.float32) * scale_factor
    grad_bias = jnp.sum(grad_pre.astype(jnp.float32), axis=0) * scale_factor
    return output, grad_features, grad_weight, grad_bias
```

```python
import jax
import jax.numpy as jnp
from jax import lax
from jax.experimental import pallas as pl
from jax.experimental.pallas import tpu as pltpu
from jax.sharding import PartitionSpec as P

BF16 = jnp.bfloat16
F32 = jnp.float32
DENSE_BYTES = 4 << 20


def dot(left, right, contract=((1,), (0,))):
    return lax.dot_general(left, right, (contract, ((), ())), preferred_element_type=F32)


def rounded(value):
    return lax.reduce_precision(value, 8, 7)


def axis_orders(loop_size):
    bits = [1 << b for b in range(loop_size.bit_length() - 1)]
    low, high = bits[: len(bits) // 2], bits[len(bits) // 2 :]
    return (high + low, high[::-1] + low[::-1])


def exchange(value, step, orders, loop_size, rep_size):
    pairs = []
    for place in range(loop_size):
        for rep in range(rep_size):
            partner = place ^ orders[rep % 2][step]
            pairs.append((place * rep_size + rep, partner * rep_size + rep))
    return lax.ppermute(value, ("loop", "rep"), pairs)


def swap_rep(value, mask, rep_size):
    return lax.ppermute(value, "rep", [(r, r ^ mask) for r in range(rep_size)])


def partner_masks(order):
    masks = [0]
    for bit in order:
        masks = masks + [m ^ bit for m in masks]
    return masks


def lay_out_kernel(row_ref, tiles_ref, near_ref, far_ref, near_t_ref, far_t_ref):
    partners, slots, tile = tiles_ref.shape[0], tiles_ref.shape[1], tiles_ref.shape[2]
    panel = near_ref.shape[0] // (slots * tile)
    half = partners // 2
    for k in range(partners):
        source = row_ref[k, slots]
        out, out_t = (near_ref, near_t_ref) if k < half else (far_ref, far_t_ref)
        cols = pl.ds((k % half) * tile, tile)
        for s in range(slots):
            one = tiles_ref[source, s]
            one_t = one.T
            for t in range(panel):
                keep = (row_ref[k, s] == t).astype(BF16)
                rows = pl.ds((s * panel + t) * tile, tile)
                out[rows, cols] = one * keep
                out_t[cols, rows] = one_t * keep


def lay_out(row_table, tiles, panel):
    partners, slots, tile, _ = tiles.shape
    wide, deep = partners // 2 * tile, slots * panel * tile
    near = jax.ShapeDtypeStruct((deep, wide), BF16)
    near_t = jax.ShapeDtypeStruct((wide, deep), BF16)
    vmem = pl.BlockSpec(memory_space=pltpu.VMEM)
    return pl.pallas_call(
        lay_out_kernel,
        out_shape=(near, near, near_t, near_t),
        in_specs=[pl.BlockSpec(memory_space=pltpu.SMEM), vmem],
        out_specs=(vmem,) * 4,
        compiler_params=pltpu.CompilerParams(vmem_limit_bytes=32 << 20),
        name="lay_out",
    )(row_table, tiles)


def body(node_features, weight, bias_vector, tile_values, tile_place, tile_count, cotangent):
    loop_size = lax.axis_size("loop")
    rep_size = lax.axis_size("rep")
    position = lax.axis_index("loop")
    rep = lax.axis_index("rep")
    rows_own, width_in = node_features.shape
    width_out = weight.shape[1]
    _, _, partners, slots, tile, _ = tile_values.shape
    per_side = rows_own // tile
    panel = rep_size * per_side
    orders = axis_orders(loop_size)
    steps = len(orders[0])
    half = partners // 2
    tiles = tile_values[0, 0]

    masks = jnp.where(
        rep % 2 == 0,
        jnp.array(partner_masks(orders[0]), jnp.int32),
        jnp.array(partner_masks(orders[1]), jnp.int32),
    )
    partner = jnp.bitwise_xor(position.astype(jnp.int32), masks)
    places = tile_place[0, 0][partner]
    target = places // per_side
    target = jnp.bitwise_xor(target // per_side, rep.astype(jnp.int32)) * per_side + target % per_side
    live = jnp.arange(slots, dtype=jnp.int32)[None, :] < tile_count[0, 0][partner][:, None]
    target = jnp.where(live, target, -1)
    dense = per_side == 1 and 2 * slots * panel * tile * partners * tile <= DENSE_BYTES

    cotangent_rows = cotangent
    for bit in range(rep_size.bit_length() - 1):
        cotangent_rows = jnp.concatenate(
            [cotangent_rows, swap_rep(cotangent_rows, 1 << bit, rep_size)], axis=0
        )

    gathered = node_features
    for step in range(steps - 1):
        gathered = jnp.concatenate(
            [gathered, exchange(gathered, step, orders, loop_size, rep_size)], axis=0
        )
    arriving = exchange(gathered, steps - 1, orders, loop_size, rep_size)

    if dense:
        table = jnp.concatenate([target, partner[:, None]], axis=1)
        near, far, near_t, far_t = lay_out(table, tiles, panel)
        both = dot(near, gathered) + dot(far, arriving)
        sums = jnp.sum(both.reshape(slots, panel * tile, width_in), axis=0)
    else:
        source = places % per_side
        everything = jnp.concatenate([gathered, arriving], axis=0)

        def forward_tile(number, totals):
            k, s = number // slots, number % slots
            right = lax.dynamic_slice_in_dim(
                everything, k * rows_own + source[k, s] * tile, tile, 0
            )
            product = dot(tiles[partner[k], s], right)
            product = product * (target[k, s] >= 0).astype(F32)
            start = jnp.maximum(target[k, s], 0) * tile
            earlier = lax.dynamic_slice_in_dim(totals, start, tile, 0)
            return lax.dynamic_update_slice_in_dim(totals, earlier + product, start, 0)

        sums = lax.fori_loop(
            0, partners * slots, forward_tile, jnp.zeros((panel * tile, width_in), F32)
        )

    for bit in range(rep_size.bit_length() - 1):
        other = swap_rep(sums, 1 << bit, rep_size)
        blocks = other.reshape(rep_size, rows_own, width_in)
        blocks = jnp.stack([blocks[t ^ (1 << bit)] for t in range(rep_size)])
        sums = sums + blocks.reshape(sums.shape)

    sums_high = rounded(sums)
    sums_low = (sums - sums_high).astype(BF16)
    sums_high = sums_high.astype(BF16)
    preact = dot(sums_high, weight) + dot(sums_low, weight) + bias_vector[None, :]
    negative = jnp.minimum(preact, 0.0)
    own = preact[:rows_own]
    output = jnp.where(own > 0, own, jnp.expm1(negative[:rows_own])).astype(BF16)
    slope = jnp.where(preact > 0, 1.0, jnp.exp(negative))
    grad_pre = (cotangent_rows.astype(F32) * slope).astype(BF16)
    grad_back = dot(grad_pre, weight, ((1,), (1,))).astype(BF16)

    share = width_in // rep_size
    own_columns = lax.dynamic_slice_in_dim(sums_high, rep * share, share, 1)
    weight_term = dot(own_columns, grad_pre, ((0,), (0,)))
    bias_term = jnp.sum(grad_pre[:rows_own].astype(F32), axis=0, keepdims=True)

    if dense:
        doubled = jnp.concatenate([grad_back] * slots, axis=0)
        sending = dot(far_t, doubled)
        keeping = dot(near_t, doubled)
    else:

        def backward_tile(number, totals):
            k, s = number // slots, number % slots
            start = jnp.maximum(target[k, s], 0) * tile
            left = lax.dynamic_slice_in_dim(grad_back, start, tile, 0)
            product = dot(tiles[partner[k], s], left, ((0,), (0,)))
            product = product * (target[k, s] >= 0).astype(F32)
            place = k * rows_own + source[k, s] * tile
            earlier = lax.dynamic_slice_in_dim(totals, place, tile, 0)
            return lax.dynamic_update_slice_in_dim(totals, earlier + product, place, 0)

        partial = lax.fori_loop(
            0, partners * slots, backward_tile, jnp.zeros((partners * rows_own, width_in), F32)
        )
        keeping, sending = partial[: half * rows_own], partial[half * rows_own :]

    for step in range(steps - 1, -1, -1):
        weight_term = rounded(weight_term)
        bias_high = rounded(bias_term)
        bias_low = rounded(bias_term - bias_high)
        blank = jnp.zeros((14, width_out), BF16)
        message = jnp.concatenate(
            [sending.astype(BF16), weight_term.astype(BF16), bias_high.astype(BF16), bias_low.astype(BF16), blank],
            axis=0,
        )
        received = exchange(message, step, orders, loop_size, rep_size).astype(F32)
        size = sending.shape[0]
        keeping = keeping + received[:size]
        weight_term = weight_term + received[size : size + share]
        tail = received[size + share :]
        bias_term = (bias_high + bias_low) + (tail[0:1] + tail[1:2])
        if step:
            keeping, sending = keeping[: size // 2], keeping[size // 2 :]
    grad_features = keeping.astype(BF16)

    scale_factor = float(rows_own * loop_size * rep_size) ** (-0.5)
    shares = jnp.concatenate(
        [weight_term, bias_term, jnp.zeros((7, width_out), F32)], axis=0
    )[None] * scale_factor
    for bit in range(rep_size.bit_length() - 1):
        shares = jnp.concatenate([shares, swap_rep(shares, 1 << bit, rep_size)], axis=0)
    by_rep = jnp.bitwise_xor(jnp.arange(rep_size, dtype=jnp.int32), rep.astype(jnp.int32))
    shares = shares[by_rep]
    grad_weight = shares[:, :share].reshape(width_in, width_out)
    grad_bias = jnp.sum(shares[:, share], axis=0)
    return (output, grad_features, grad_weight, grad_bias)


def solution(mesh):
    return jax.shard_map(
        body,
        mesh=mesh,
        in_specs=(
            P(("loop", "rep"), None),
            P(),
            P(),
            P("loop", "rep", None, None, None, None),
            P("loop", "rep", None, None),
            P("loop", "rep", None),
            P(("loop", "rep"), None),
        ),
        out_specs=(P(("loop", "rep"), None), P(("loop", "rep"), None), P(), P()),
        check_vma=False,
    )
```

```python
from functools import partial

import jax
import jax.numpy as jnp
from jax import lax
from jax.experimental import pallas as pl
from jax.experimental.pallas import tpu as pltpu
from jax.sharding import PartitionSpec as P

BF16 = jnp.bfloat16
F32 = jnp.float32
DENSE_BYTES = 4 << 20


def dot(left, right, contract=((1,), (0,))):
    return lax.dot_general(left, right, (contract, ((), ())), preferred_element_type=F32)


def axis_orders(loop_size):
    bits = [1 << b for b in range(loop_size.bit_length() - 1)]
    low, high = bits[: len(bits) // 2], bits[len(bits) // 2 :]
    return (high + low, high[::-1] + low[::-1])


def exchange(value, step, orders, loop_size, rep_size):
    pairs = []
    for place in range(loop_size):
        for rep in range(rep_size):
            partner = place ^ orders[rep % 2][step]
            pairs.append((place * rep_size + rep, partner * rep_size + rep))
    return lax.ppermute(value, ("loop", "rep"), pairs)


def swap_rep(value, mask, rep_size):
    return lax.ppermute(value, "rep", [(r, r ^ mask) for r in range(rep_size)])


def partner_masks(order):
    masks = [0]
    for bit in order:
        masks = masks + [m ^ bit for m in masks]
    return masks


def scatter_tiles(row_ref, tiles_ref, k, out, out_t, first):
    slots, tile = tiles_ref.shape[1], tiles_ref.shape[2]
    panel = out_t.shape[1] // (slots * tile)
    source = row_ref[k, slots]
    cols = pl.ds((k - first) * tile, tile)
    for s in range(slots):
        one = tiles_ref[source, s]
        one_t = one.T
        for t in range(panel):
            keep = (row_ref[k, s] == t).astype(BF16)
            rows = pl.ds((s * panel + t) * tile, tile)
            out[rows, cols] = one * keep
            out_t[cols, rows] = one_t * keep


def fold(both):
    half = both.shape[0] // 2
    return both[:half] + both[half:]


def near_kernel(row_ref, tiles_ref, right_ref, sums_ref, far_ref, near_t_ref, far_t_ref, near_ref):
    partners = tiles_ref.shape[0]
    half = partners // 2
    for k in range(half):
        scatter_tiles(row_ref, tiles_ref, k, near_ref, near_t_ref, 0)
    sums_ref[...] = fold(dot(near_ref[...], right_ref[...]))
    for k in range(half, partners):
        scatter_tiles(row_ref, tiles_ref, k, far_ref, far_t_ref, half)


def far_kernel(sums_ref, far_ref, right_ref, out_ref):
    out_ref[...] = sums_ref[...] + fold(dot(far_ref[...], right_ref[...]))


def split(value):
    high = value.astype(BF16)
    return high, (value - high.astype(F32)).astype(BF16)


def exp_less_one(value, grown):
    series = value * (1.0 + value * (1 / 2 + value * (1 / 6 + value * (1 / 24))))
    return jnp.where(value > -0.0625, series, grown - 1.0)


def middle_kernel(
    mine_ref, other_ref, weight_ref, bias_ref, own_ref, pair_ref, far_t_ref,
    message_ref, output_ref, back_ref, grad_ref, sums_ref,
):
    rows = own_ref.shape[0]
    sums_ref[:rows] = mine_ref[:rows] + other_ref[rows:]
    sums_ref[rows:] = mine_ref[rows:] + other_ref[:rows]
    high, low = split(sums_ref[...])
    weight = weight_ref[...]
    preact = dot(high, weight) + dot(low, weight) + bias_ref[...]
    negative = jnp.minimum(preact, 0.0)
    grown = jnp.exp(negative)
    slope = jnp.where(preact > 0, 1.0, grown)
    own = preact[:rows]
    below = exp_less_one(negative[:rows], grown[:rows])
    output_ref[...] = jnp.where(own > 0, own, below).astype(BF16)
    grad_ref[:rows] = (own_ref[...].astype(F32) * slope[:rows]).astype(BF16)
    grad_ref[rows:] = (pair_ref[...].astype(F32) * slope[rows:]).astype(BF16)
    back = dot(grad_ref[...], weight, ((1,), (1,))).astype(BF16)
    back_ref[: 2 * rows] = back
    back_ref[2 * rows :] = back
    message_ref[...] = dot(far_t_ref[...], back_ref[...]).astype(BF16)


def keep_kernel(rep_ref, near_t_ref, back_ref, grad_ref, sums_ref, keep_ref, term_ref):
    share = term_ref.shape[0] - 8
    sums = sums_ref[...]
    mine = jnp.where(rep_ref[0, 0] == 0, sums[:, :share], sums[:, share:])
    high, low = split(mine)
    grad = grad_ref[...]
    rows = ((0,), (0,))
    term_ref[:share] = dot(high, grad, rows) + dot(low, grad, rows)
    own = grad[: grad.shape[0] // 2].astype(F32)
    term_ref[share:] = jnp.broadcast_to(jnp.sum(own, axis=0, keepdims=True), (8, own.shape[1]))
    keep_ref[...] = dot(near_t_ref[...], back_ref[...])


def final_kernel(rep_ref, mine_ref, other_ref, weight_ref, bias_ref, *, scale):
    share = weight_ref.shape[0] // 2
    mine, other = mine_ref[...] * scale, other_ref[...] * scale
    first = rep_ref[0, 0] == 0
    weight_ref[:share] = jnp.where(first, mine[:share], other[:share])
    weight_ref[share:] = jnp.where(first, other[:share], mine[:share])
    bias_ref[...] = mine[share : share + 1] + other[share : share + 1]


def on_chip(kernel, shapes, scratch=(), scalars=0):
    vmem = pl.BlockSpec(memory_space=pltpu.VMEM)
    smem = pl.BlockSpec(memory_space=pltpu.SMEM)

    def call(*operands):
        return pl.pallas_call(
            kernel,
            out_shape=tuple(jax.ShapeDtypeStruct(*shape) for shape in shapes),
            in_specs=[smem] * scalars + [vmem] * (len(operands) - scalars),
            out_specs=(vmem,) * len(shapes),
            scratch_shapes=list(scratch),
            compiler_params=pltpu.CompilerParams(vmem_limit_bytes=40 << 20),
        )(*operands)

    return call


def tile_loop(target, source, partner, tiles, totals, right_of, product_of, place_of):
    slots = tiles.shape[1]

    def one(number, totals):
        k, s = number // slots, number % slots
        product = product_of(tiles[partner[k], s], right_of(k, s))
        product = product * (target[k, s] >= 0).astype(F32)
        start = place_of(k, s)
        earlier = lax.dynamic_slice_in_dim(totals, start, product.shape[0], 0)
        return lax.dynamic_update_slice_in_dim(totals, earlier + product, start, 0)

    return lax.fori_loop(0, target.shape[0] * slots, one, totals)


def body(node_features, weight, bias_vector, tile_values, tile_place, tile_count, cotangent):
    loop_size = lax.axis_size("loop")
    rep_size = lax.axis_size("rep")
    position = lax.axis_index("loop").astype(jnp.int32)
    rep = lax.axis_index("rep").astype(jnp.int32)
    rows_own, width_in = node_features.shape
    width_out = weight.shape[1]
    _, _, partners, slots, tile, _ = tile_values.shape
    per_side = rows_own // tile
    panel = rep_size * per_side
    orders = axis_orders(loop_size)
    steps = len(orders[0])
    half = partners // 2
    share = width_in // rep_size
    scale_factor = float(rows_own * loop_size * rep_size) ** (-0.5)
    tiles = tile_values[0, 0]
    rep_bits = [1 << bit for bit in range(rep_size.bit_length() - 1)]
    dense_bytes = 2 * slots * panel * tile * partners * tile
    dense = per_side == 1 and rep_size == 2 and slots == 2 and dense_bytes <= DENSE_BYTES

    masks = jnp.where(
        rep % 2 == 0,
        jnp.array(partner_masks(orders[0]), jnp.int32),
        jnp.array(partner_masks(orders[1]), jnp.int32),
    )
    partner = jnp.bitwise_xor(position, masks)
    places = tile_place[0, 0][partner]
    target = places // per_side
    target = jnp.bitwise_xor(target // per_side, rep) * per_side + target % per_side
    live = jnp.arange(slots, dtype=jnp.int32)[None, :] < tile_count[0, 0][partner][:, None]
    target = jnp.where(live, target, -1)

    gathered = node_features
    for step in range(steps - 1):
        gathered = jnp.concatenate(
            [gathered, exchange(gathered, step, orders, loop_size, rep_size)], axis=0
        )
    arriving = exchange(gathered, steps - 1, orders, loop_size, rep_size)

    cotangent_rows = [cotangent]
    for bit in rep_bits:
        cotangent_rows += [swap_rep(rows, bit, rep_size) for rows in cotangent_rows]

    if dense:
        table = jnp.concatenate([target, partner[:, None]], axis=1)
        wide, deep, rows = half * tile, slots * panel * tile, panel * tile
        rep_word = rep.reshape(1, 1)
        sums, far, near_t, far_t = on_chip(
            near_kernel,
            [((rows, width_in), F32), ((deep, wide), BF16), ((wide, deep), BF16), ((wide, deep), BF16)],
            [pltpu.VMEM((deep, wide), BF16)],
            1,
        )(table, tiles, gathered)
        (sums,) = on_chip(far_kernel, [((rows, width_in), F32)])(sums, far, arriving)
        other = swap_rep(sums, 1, rep_size)
        sending, output, back, grad_pre, sums = on_chip(
            middle_kernel,
            [
                ((wide, width_in), BF16),
                ((rows_own, width_out), BF16),
                ((slots * rows, width_in), BF16),
                ((rows, width_out), BF16),
                ((rows, width_in), F32),
            ],
        )(sums, other, weight, bias_vector.reshape(1, width_out), *cotangent_rows, far_t)
        keeping, term = on_chip(
            keep_kernel, [((wide, width_in), F32), ((share + 8, width_out), F32)], (), 1
        )(rep_word, near_t, back, grad_pre, sums)
    else:
        source = places % per_side
        everything = jnp.concatenate([gathered, arriving], axis=0)
        sums = tile_loop(
            target, source, partner, tiles, jnp.zeros((panel * tile, width_in), F32),
            lambda k, s: lax.dynamic_slice_in_dim(
                everything, k * rows_own + source[k, s] * tile, tile, 0
            ),
            dot,
            lambda k, s: jnp.maximum(target[k, s], 0) * tile,
        )
        for bit in rep_bits:
            other = swap_rep(sums, bit, rep_size)
            blocks = other.reshape(rep_size, rows_own, width_in)
            blocks = jnp.stack([blocks[t ^ bit] for t in range(rep_size)])
            sums = sums + blocks.reshape(sums.shape)
        high = lax.reduce_precision(sums, 8, 7)
        low = (sums - high).astype(BF16)
        high = high.astype(BF16)
        preact = dot(high, weight) + dot(low, weight) + bias_vector[None, :]
        negative = jnp.minimum(preact, 0.0)
        own = preact[:rows_own]
        output = jnp.where(own > 0, own, jnp.expm1(negative[:rows_own])).astype(BF16)
        slope = jnp.where(preact > 0, 1.0, jnp.exp(negative))
        cotangent_rows = jnp.concatenate(cotangent_rows, axis=0)
        grad_pre = (cotangent_rows.astype(F32) * slope).astype(BF16)
        back = dot(grad_pre, weight, ((1,), (1,))).astype(BF16)
        start = rep * share
        term = dot(lax.dynamic_slice_in_dim(high, start, share, 1), grad_pre, ((0,), (0,)))
        term = term + dot(lax.dynamic_slice_in_dim(low, start, share, 1), grad_pre, ((0,), (0,)))
        bias_term = jnp.sum(grad_pre[:rows_own].astype(F32), axis=0, keepdims=True)
        term = jnp.concatenate([term, jnp.broadcast_to(bias_term, (8, width_out))], axis=0)
        adjoint = tile_loop(
            target, source, partner, tiles, jnp.zeros((partners * rows_own, width_in), F32),
            lambda k, s: lax.dynamic_slice_in_dim(
                back, jnp.maximum(target[k, s], 0) * tile, tile, 0
            ),
            lambda left, right: dot(left, right, ((0,), (0,))),
            lambda k, s: k * rows_own + source[k, s] * tile,
        )
        keeping, sending = adjoint[: half * rows_own], adjoint[half * rows_own :].astype(BF16)

    received = []
    for step in range(steps - 1, -1, -1):
        received.append(exchange(sending, step, orders, loop_size, rep_size))
        term = term + exchange(term, (step + steps // 2) % steps, orders, loop_size, rep_size)
        size = sending.shape[0] // 2 if step else 0
        end = 2 * size if step else rows_own
        total = keeping[size:end]
        for part in received:
            total = total + part[size:end].astype(F32)
        sending = total.astype(BF16)
    grad_features = sending

    if dense:
        grad_weight, grad_bias = on_chip(
            partial(final_kernel, scale=scale_factor),
            [((width_in, width_out), F32), ((1, width_out), F32)],
            (),
            1,
        )(rep_word, term, swap_rep(term, 1, rep_size))
        grad_bias = grad_bias.reshape(width_out)
    else:
        shares = term[None] * scale_factor
        for bit in rep_bits:
            shares = jnp.concatenate([shares, swap_rep(shares, bit, rep_size)], axis=0)
        shares = shares[jnp.bitwise_xor(jnp.arange(rep_size, dtype=jnp.int32), rep)]
        grad_weight = shares[:, :share].reshape(width_in, width_out)
        grad_bias = jnp.sum(shares[:, share], axis=0)
    return (output, grad_features, grad_weight, grad_bias)


def solution(mesh):
    return jax.shard_map(
        body,
        mesh=mesh,
        in_specs=(
            P(("loop", "rep"), None),
            P(),
            P(),
            P("loop", "rep", None, None, None, None),
            P("loop", "rep", None, None),
            P("loop", "rep", None),
            P(("loop", "rep"), None),
        ),
        out_specs=(P(("loop", "rep"), None), P(("loop", "rep"), None), P(), P()),
        check_vma=False,
    )
```

```python
from functools import partial

import jax
import jax.numpy as jnp
from jax import lax
from jax.experimental import pallas as pl
from jax.experimental.pallas import tpu as pltpu
from jax.sharding import PartitionSpec as P

BF16 = jnp.bfloat16
F32 = jnp.float32


def dot(left, right, contract=((1,), (0,))):
    return lax.dot_general(left, right, (contract, ((), ())), preferred_element_type=F32)


def axis_order(loop_size):
    bits = [1 << b for b in range(loop_size.bit_length() - 1)]
    low, high = bits[: len(bits) // 2], bits[len(bits) // 2 :]
    return high[::-1] + low


def exchange(value, masks, loop_size, rep_size):
    pairs = []
    for place in range(loop_size):
        for rep in range(rep_size):
            partner = place ^ masks[rep % 2]
            pairs.append((place * rep_size + rep, partner * rep_size + rep))
    return lax.ppermute(value, ("loop", "rep"), pairs)


def swap_rep(value, mask, rep_size):
    return lax.ppermute(value, "rep", [(r, r ^ mask) for r in range(rep_size)])


def partner_masks(order):
    masks = [0]
    for bit in order:
        masks = masks + [m ^ bit for m in masks]
    return masks


def scatter_tiles(word_ref, place_ref, count_ref, masks, tiles_ref, k, out, out_t, first):
    slots, tile = tiles_ref.shape[1], tiles_ref.shape[2]
    panel = out_t.shape[1] // (slots * tile)
    rep = word_ref[0, 1]
    mask = jnp.where(rep == 0, masks[0][k], masks[1][k])
    source = jnp.bitwise_xor(word_ref[0, 0], mask)
    count = count_ref[0, source]
    cols = pl.ds((k - first) * tile, tile)
    for s in range(slots):
        one = tiles_ref[source, s]
        one_t = one.T
        row = jnp.where(s < count, jnp.bitwise_xor(place_ref[source, s], rep), -1)
        for t in range(panel):
            keep = (row == t).astype(BF16)
            rows = pl.ds((s * panel + t) * tile, tile)
            out[rows, cols] = one * keep
            out_t[cols, rows] = one_t * keep


def fold(both):
    half = both.shape[0] // 2
    return both[:half] + both[half:]


def near_kernel(
    word_ref, place_ref, count_ref, tiles_ref, own_ref, come_ref,
    sums_ref, far_ref, near_t_ref, far_t_ref, near_ref, *, masks,
):
    lists = (word_ref, place_ref, count_ref, masks, tiles_ref)
    partners = tiles_ref.shape[0]
    half = partners // 2
    for k in range(half):
        scatter_tiles(*lists, k, near_ref, near_t_ref, 0)
    wide = own_ref.shape[0]
    sums_ref[...] = fold(dot(near_ref[:, :wide], own_ref[...]) + dot(near_ref[:, wide:], come_ref[...]))
    for k in range(half, partners):
        scatter_tiles(*lists, k, far_ref, far_t_ref, half)


def far_kernel(sums_ref, far_ref, own_ref, come_ref, out_ref):
    wide = own_ref.shape[0]
    both = dot(far_ref[:, :wide], own_ref[...]) + dot(far_ref[:, wide:], come_ref[...])
    out_ref[...] = sums_ref[...] + fold(both)


def split(value):
    high = value.astype(BF16)
    return high, (value - high.astype(F32)).astype(BF16)


def exp_less_one(value, grown):
    series = value * (1.0 + value * (1 / 2 + value * (1 / 6 + value * (1 / 24))))
    return jnp.where(value > -0.0625, series, grown - 1.0)


def middle_kernel(
    mine_ref, other_ref, weight_ref, bias_ref, own_ref, pair_ref, far_t_ref,
    message_ref, output_ref, back_ref, grad_ref, sums_ref,
):
    rows = own_ref.shape[0]
    sums_ref[:rows] = mine_ref[:rows] + other_ref[rows:]
    sums_ref[rows:] = mine_ref[rows:] + other_ref[:rows]
    high, low = split(sums_ref[...])
    weight = weight_ref[...]
    preact = dot(high, weight) + dot(low, weight) + bias_ref[...]
    negative = jnp.minimum(preact, 0.0)
    grown = jnp.exp(negative)
    slope = jnp.where(preact > 0, 1.0, grown)
    own = preact[:rows]
    below = exp_less_one(negative[:rows], grown[:rows])
    output_ref[...] = jnp.where(own > 0, own, below).astype(BF16)
    grad_ref[:rows] = (own_ref[...].astype(F32) * slope[:rows]).astype(BF16)
    grad_ref[rows:] = (pair_ref[...].astype(F32) * slope[rows:]).astype(BF16)
    back = dot(grad_ref[...], weight, ((1,), (1,))).astype(BF16)
    back_ref[: 2 * rows] = back
    back_ref[2 * rows :] = back
    wide = message_ref.shape[0]
    message_ref[...] = dot(far_t_ref[wide:], back_ref[...]).astype(BF16)


def message_kernel(near_t_ref, back_ref, message_ref):
    wide = message_ref.shape[0]
    message_ref[...] = dot(near_t_ref[wide:], back_ref[...]).astype(BF16)


def pack_terms(out_ref, weight_term, bias_term):
    share = weight_term.shape[0]
    out_ref[:share] = weight_term.astype(BF16)
    high, low = split(bias_term)
    row = lax.broadcasted_iota(jnp.int32, (16, bias_term.shape[1]), 0)
    low = jnp.where(row == 1, low.astype(F32), 0.0)
    out_ref[share:] = jnp.where(row == 0, high.astype(F32), low).astype(BF16)


def add_packed(mine_ref, other_ref):
    total = mine_ref[...].astype(F32) + other_ref[...].astype(F32)
    share = total.shape[0] - 16
    return total[:share], total[share : share + 1] + total[share + 1 : share + 2]


def repack_kernel(mine_ref, other_ref, out_ref):
    pack_terms(out_ref, *add_packed(mine_ref, other_ref))


def unpack_kernel(mine_ref, other_ref, out_ref):
    weight_term, bias_term = add_packed(mine_ref, other_ref)
    share = weight_term.shape[0]
    out_ref[:share] = weight_term
    out_ref[share:] = jnp.broadcast_to(bias_term, (8, bias_term.shape[1]))


def keep_kernel(word_ref, near_t_ref, far_t_ref, back_ref, grad_ref, sums_ref, near_ref, far_ref, term_ref):
    share = term_ref.shape[0] - 16
    sums = sums_ref[...]
    mine = jnp.where(word_ref[0, 1] == 0, sums[:, :share], sums[:, share:])
    high, low = split(mine)
    grad = grad_ref[...]
    rows = ((0,), (0,))
    own = jnp.sum(grad[: grad.shape[0] // 2].astype(F32), axis=0, keepdims=True)
    pack_terms(term_ref, dot(high, grad, rows) + dot(low, grad, rows), own)
    wide = near_ref.shape[0]
    far_ref[...] = dot(far_t_ref[:wide], back_ref[...])
    near_ref[...] = dot(near_t_ref[:wide], back_ref[...])


def final_kernel(word_ref, mine_ref, other_ref, weight_ref, bias_ref, *, scale):
    share = weight_ref.shape[0] // 2
    mine, other = mine_ref[...] * scale, other_ref[...] * scale
    first = word_ref[0, 1] == 0
    weight_ref[:share] = jnp.where(first, mine[:share], other[:share])
    weight_ref[share:] = jnp.where(first, other[:share], mine[:share])
    bias_ref[...] = mine[share : share + 1] + other[share : share + 1]


def on_chip(kernel, shapes, scratch=(), scalars=0):
    vmem = pl.BlockSpec(memory_space=pltpu.VMEM)
    smem = pl.BlockSpec(memory_space=pltpu.SMEM)

    def call(*operands):
        return pl.pallas_call(
            kernel,
            out_shape=tuple(jax.ShapeDtypeStruct(*shape) for shape in shapes),
            in_specs=[smem] * scalars + [vmem] * (len(operands) - scalars),
            out_specs=(vmem,) * len(shapes),
            scratch_shapes=list(scratch),
            compiler_params=pltpu.CompilerParams(vmem_limit_bytes=40 << 20),
        )(*operands)

    return call


def tile_loop(target, source, partner, tiles, totals, right_of, product_of, place_of):
    slots = tiles.shape[1]

    def one(number, totals):
        k, s = number // slots, number % slots
        product = product_of(tiles[partner[k], s], right_of(k, s))
        product = product * (target[k, s] >= 0).astype(F32)
        start = place_of(k, s)
        earlier = lax.dynamic_slice_in_dim(totals, start, product.shape[0], 0)
        return lax.dynamic_update_slice_in_dim(totals, earlier + product, start, 0)

    return lax.fori_loop(0, target.shape[0] * slots, one, totals)


def slot_targets(tile_place, tile_count, partner, rep, per_side):
    places = tile_place[0, 0][partner]
    target = places // per_side
    target = jnp.bitwise_xor(target // per_side, rep) * per_side + target % per_side
    slots = places.shape[1]
    live = jnp.arange(slots, dtype=jnp.int32)[None, :] < tile_count[0, 0][partner][:, None]
    return jnp.where(live, target, -1), places % per_side


def plus(*parts):
    total = None
    for part, start, size in parts:
        rows = part[start : start + size].astype(F32)
        total = rows if total is None else total + rows
    return total


def after(value, *others):
    return lax.optimization_barrier((value, others))[0]


def dense_body(node_features, weight, bias_vector, tile_values, tile_place, tile_count, cotangent):
    loop_size = lax.axis_size("loop")
    position = lax.axis_index("loop").astype(jnp.int32)
    rep = lax.axis_index("rep").astype(jnp.int32)
    rows_own, width_in = node_features.shape
    width_out = weight.shape[1]
    _, _, partners, slots, tile, _ = tile_values.shape
    share = width_in // 2
    scale_factor = float(rows_own * loop_size * 2) ** (-0.5)
    wide, deep, rows = partners // 2 * tile, slots * 2 * tile, 2 * tile

    def move(value, masks):
        return exchange(value, masks, loop_size, 2)

    far_z, near_z, first, second = (8, 8), (4, 4), (1, 2), (2, 1)
    masks = [
        partner_masks([far_z[core], first[core], second[core], near_z[core]]) for core in range(2)
    ]
    words = jnp.stack([position, rep]).reshape(1, 2)

    own_near = jnp.concatenate([node_features, move(node_features, far_z)], axis=0)
    own_far = move(own_near, near_z)
    own_near = jnp.concatenate([own_near, move(own_near, first)], axis=0)
    come_near = move(own_near, second)
    own_far = jnp.concatenate([own_far, move(own_far, first)], axis=0)
    come_far = move(own_far, second)
    pair_cotangent = swap_rep(cotangent, 1, 2)

    sums, far, near_t, far_t = on_chip(
        partial(near_kernel, masks=masks),
        [((rows, width_in), F32), ((deep, wide), BF16), ((wide, deep), BF16), ((wide, deep), BF16)],
        [pltpu.VMEM((deep, wide), BF16)],
        3,
    )(words, tile_place[0, 0], tile_count[0], tile_values[0, 0], own_near, come_near)
    (sums,) = on_chip(far_kernel, [((rows, width_in), F32)])(sums, far, own_far, come_far)
    far_message, output, back, grad_pre, sums = on_chip(
        middle_kernel,
        [
            ((wide // 2, width_in), BF16),
            ((rows_own, width_out), BF16),
            ((slots * rows, width_in), BF16),
            ((rows, width_out), BF16),
            ((rows, width_in), F32),
        ],
    )(sums, swap_rep(sums, 1, 2), weight, bias_vector.reshape(1, width_out), cotangent, pair_cotangent, far_t)
    (near_message,) = on_chip(message_kernel, [((wide // 2, width_in), BF16)])(near_t, back)
    near_keep, far_keep, term = on_chip(
        keep_kernel,
        [((wide // 2, width_in), F32), ((wide // 2, width_in), F32), ((share + 16, width_out), BF16)],
        (),
        1,
    )(words, near_t, far_t, back, grad_pre, sums)

    far_1 = move(far_message, second)
    near_1 = move(near_message, second)
    (term,) = on_chip(repack_kernel, [(term.shape, BF16)])(term, move(term, (4, 8)))
    half, one = wide // 4, rows_own
    far_message = plus((far_keep, half, half), (far_1, half, half)).astype(BF16)
    far_2 = move(far_message, first)
    near_message = plus((near_keep, half, half), (near_1, half, half)).astype(BF16)
    near_2 = move(near_message, first)
    term = after(term, far_1)
    (term,) = on_chip(unpack_kernel, [((share + 8, width_out), F32)])(term, move(term, (8, 4)))
    z_message = plus((far_keep, 0, half), (far_1, 0, half), (far_2, 0, half)).astype(BF16)
    far_3 = move(z_message, near_z)
    near_parts = (near_keep, near_1, near_2, far_3)
    term = after(term, near_1)
    term = term + move(term, (1, 2))
    last_message = plus(*((part, one, one) for part in near_parts)).astype(BF16)
    last = move(last_message, far_z)
    term = after(term, far_2, near_2)
    term = term + move(term, (2, 1))
    grad_features = plus(*((part, 0, one) for part in near_parts), (last, 0, one)).astype(BF16)

    grad_weight, grad_bias = on_chip(
        partial(final_kernel, scale=scale_factor),
        [((width_in, width_out), F32), ((1, width_out), F32)],
        (),
        1,
    )(words, term, swap_rep(term, 1, 2))
    return (output, grad_features, grad_weight, grad_bias.reshape(width_out))


def general_body(node_features, weight, bias_vector, tile_values, tile_place, tile_count, cotangent):
    loop_size = lax.axis_size("loop")
    rep_size = lax.axis_size("rep")
    position = lax.axis_index("loop").astype(jnp.int32)
    rep = lax.axis_index("rep").astype(jnp.int32)
    rows_own, width_in = node_features.shape
    width_out = weight.shape[1]
    partners, tile = tile_values.shape[2], tile_values.shape[4]
    per_side = rows_own // tile
    panel = rep_size * per_side
    order = axis_order(loop_size)
    half = partners // 2
    share = width_in // rep_size
    scale_factor = float(rows_own * loop_size * rep_size) ** (-0.5)
    tiles = tile_values[0, 0]
    rep_bits = [1 << bit for bit in range(rep_size.bit_length() - 1)]
    partner = jnp.bitwise_xor(position, jnp.array(partner_masks(order), jnp.int32))
    target, source = slot_targets(tile_place, tile_count, partner, rep, per_side)

    def move(value, bit):
        return exchange(value, (bit, bit), loop_size, rep_size)

    gathered = node_features
    for bit in order:
        gathered = jnp.concatenate([gathered, move(gathered, bit)], axis=0)
    cotangent_rows = cotangent
    for bit in rep_bits:
        cotangent_rows = jnp.concatenate(
            [cotangent_rows, swap_rep(cotangent_rows, bit, rep_size)], axis=0
        )
    sums = tile_loop(
        target, source, partner, tiles, jnp.zeros((panel * tile, width_in), F32),
        lambda k, s: lax.dynamic_slice_in_dim(
            gathered, k * rows_own + source[k, s] * tile, tile, 0
        ),
        dot,
        lambda k, s: jnp.maximum(target[k, s], 0) * tile,
    )
    for bit in rep_bits:
        other = swap_rep(sums, bit, rep_size)
        blocks = other.reshape(rep_size, rows_own, width_in)
        blocks = jnp.stack([blocks[t ^ bit] for t in range(rep_size)])
        sums = sums + blocks.reshape(sums.shape)
    high = lax.reduce_precision(sums, 8, 7)
    low = (sums - high).astype(BF16)
    high = high.astype(BF16)
    preact = dot(high, weight) + dot(low, weight) + bias_vector[None, :]
    negative = jnp.minimum(preact, 0.0)
    own = preact[:rows_own]
    output = jnp.where(own > 0, own, jnp.expm1(negative[:rows_own])).astype(BF16)
    slope = jnp.where(preact > 0, 1.0, jnp.exp(negative))
    grad_pre = (cotangent_rows.astype(F32) * slope).astype(BF16)
    back = dot(grad_pre, weight, ((1,), (1,))).astype(BF16)
    start = rep * share
    term = dot(lax.dynamic_slice_in_dim(high, start, share, 1), grad_pre, ((0,), (0,)))
    term = term + dot(lax.dynamic_slice_in_dim(low, start, share, 1), grad_pre, ((0,), (0,)))
    bias_term = jnp.sum(grad_pre[:rows_own].astype(F32), axis=0, keepdims=True)
    term = jnp.concatenate([term, jnp.broadcast_to(bias_term, (8, width_out))], axis=0)
    adjoint = tile_loop(
        target, source, partner, tiles, jnp.zeros((partners * rows_own, width_in), F32),
        lambda k, s: lax.dynamic_slice_in_dim(back, jnp.maximum(target[k, s], 0) * tile, tile, 0),
        lambda left, right: dot(left, right, ((0,), (0,))),
        lambda k, s: k * rows_own + source[k, s] * tile,
    )
    size = half * rows_own
    for bit in order[::-1]:
        term = term + move(term, bit)
        adjoint = adjoint[:size] + move(adjoint[size:].astype(BF16), bit).astype(F32)
        size = size // 2
    shares = term[None] * scale_factor
    for bit in rep_bits:
        shares = jnp.concatenate([shares, swap_rep(shares, bit, rep_size)], axis=0)
    shares = shares[jnp.bitwise_xor(jnp.arange(rep_size, dtype=jnp.int32), rep)]
    grad_weight = shares[:, :share].reshape(width_in, width_out)
    return (output, adjoint.astype(BF16), grad_weight, jnp.sum(shares[:, share], axis=0))


def body(*arrays):
    rows_own, tile_values = arrays[0].shape[0], arrays[3]
    _, _, partners, slots, tile, _ = tile_values.shape
    groups = (lax.axis_size("rep"), partners, slots, rows_own // tile)
    return (dense_body if groups == (2, 16, 2, 1) else general_body)(*arrays)


def solution(mesh):
    return jax.shard_map(
        body,
        mesh=mesh,
        in_specs=(
            P(("loop", "rep"), None),
            P(),
            P(),
            P("loop", "rep", None, None, None, None),
            P("loop", "rep", None, None),
            P("loop", "rep", None),
            P(("loop", "rep"), None),
        ),
        out_specs=(P(("loop", "rep"), None), P(("loop", "rep"), None), P(), P()),
        check_vma=False,
    )
```

```python
from functools import partial

import jax
import jax.numpy as jnp
from jax import lax
from jax.experimental import pallas as pl
from jax.experimental.pallas import tpu as pltpu
from jax.sharding import PartitionSpec as P

BF16 = jnp.bfloat16
F32 = jnp.float32


def dot(left, right, contract=((1,), (0,))):
    return lax.dot_general(left, right, (contract, ((), ())), preferred_element_type=F32)


def axis_order(loop_size):
    bits = [1 << b for b in range(loop_size.bit_length() - 1)]
    low, high = bits[: len(bits) // 2], bits[len(bits) // 2 :]
    return high[::-1] + low


def exchange(value, masks, loop_size, rep_size):
    pairs = []
    for place in range(loop_size):
        for rep in range(rep_size):
            partner = place ^ masks[rep % 2]
            pairs.append((place * rep_size + rep, partner * rep_size + rep))
    return lax.ppermute(value, ("loop", "rep"), pairs)


def swap_rep(value, mask, rep_size):
    return lax.ppermute(value, "rep", [(r, r ^ mask) for r in range(rep_size)])


def partner_masks(order):
    masks = [0]
    for bit in order:
        masks = masks + [m ^ bit for m in masks]
    return masks


def scatter_tiles(position_ref, rep_ref, place_ref, count_ref, masks, tiles_ref, k, out, out_t, first):
    slots, tile = tiles_ref.shape[1], tiles_ref.shape[2]
    panel = out_t.shape[1] // (slots * tile)
    rep = rep_ref[0, 0]
    mask = jnp.where(rep == 0, masks[0][k], masks[1][k])
    source = jnp.bitwise_xor(position_ref[0, 0], mask)
    count = count_ref[0, source]
    cols = pl.ds((k - first) * tile, tile)
    for s in range(slots):
        one = tiles_ref[source, s]
        one_t = one.T
        row = jnp.where(s < count, jnp.bitwise_xor(place_ref[source, s], rep), -1)
        for t in range(panel):
            keep = (row == t).astype(BF16)
            rows = pl.ds((s * panel + t) * tile, tile)
            out[rows, cols] = one * keep
            out_t[cols, rows] = one_t * keep


def fold(both):
    half = both.shape[0] // 2
    return both[:half] + both[half:]


def near_kernel(
    position_ref, rep_ref, place_ref, count_ref, tiles_ref, own_ref, come_ref,
    cotangent_ref, pair_ref, weight_ref, bias_ref,
    sums_ref, far_ref, near_t_ref, far_t_ref, panel_ref, weight_out_ref, bias_out_ref, near_ref, *, masks,
):
    lists = (position_ref, rep_ref, place_ref, count_ref, masks, tiles_ref)
    partners = tiles_ref.shape[0]
    half = partners // 2
    for k in range(half):
        scatter_tiles(*lists, k, near_ref, near_t_ref, 0)
    wide = own_ref.shape[0]
    sums_ref[...] = fold(dot(near_ref[:, :wide], own_ref[...]) + dot(near_ref[:, wide:], come_ref[...]))
    for k in range(half, partners):
        scatter_tiles(*lists, k, far_ref, far_t_ref, half)
    rows = cotangent_ref.shape[0]
    panel_ref[:rows] = cotangent_ref[...]
    panel_ref[rows:] = pair_ref[...]
    weight_out_ref[...] = weight_ref[...]
    bias_out_ref[...] = bias_ref[...]


def far_kernel(sums_ref, far_ref, own_ref, come_ref, out_ref):
    wide = own_ref.shape[0]
    both = dot(far_ref[:, :wide], own_ref[...]) + dot(far_ref[:, wide:], come_ref[...])
    out_ref[...] = sums_ref[...] + fold(both)


def split(value):
    high = value.astype(BF16)
    return high, (value - high.astype(F32)).astype(BF16)


def exp_less_one(value, grown):
    series = value * (1.0 + value * (1 / 2 + value * (1 / 6 + value * (1 / 24))))
    return jnp.where(value > -0.0625, series, grown - 1.0)


def middle_kernel(
    mine_ref, other_ref, weight_ref, bias_ref, panel_ref, far_t_ref,
    message_ref, output_ref, back_ref, grad_ref, sums_ref,
):
    rows = output_ref.shape[0]
    sums_ref[:rows] = mine_ref[:rows] + other_ref[rows:]
    sums_ref[rows:] = mine_ref[rows:] + other_ref[:rows]
    high, low = split(sums_ref[...])
    weight = weight_ref[...]
    preact = dot(high, weight) + dot(low, weight) + bias_ref[...]
    negative = jnp.minimum(preact, 0.0)
    grown = jnp.exp(negative)
    slope = jnp.where(preact > 0, 1.0, grown)
    own = preact[:rows]
    below = exp_less_one(negative[:rows], grown[:rows])
    output_ref[...] = jnp.where(own > 0, own, below).astype(BF16)
    grad_ref[...] = (panel_ref[...].astype(F32) * slope).astype(BF16)
    back = dot(grad_ref[...], weight, ((1,), (1,))).astype(BF16)
    back_ref[: 2 * rows] = back
    back_ref[2 * rows :] = back
    wide = message_ref.shape[0]
    message_ref[...] = dot(far_t_ref[wide:], back_ref[...]).astype(BF16)


def message_kernel(near_t_ref, back_ref, message_ref):
    wide = message_ref.shape[0]
    message_ref[...] = dot(near_t_ref[wide:], back_ref[...]).astype(BF16)


def pack_terms(out_ref, weight_term, bias_term):
    share = weight_term.shape[0]
    out_ref[:share] = weight_term.astype(BF16)
    high, low = split(bias_term)
    row = lax.broadcasted_iota(jnp.int32, (16, bias_term.shape[1]), 0)
    low = jnp.where(row == 1, low.astype(F32), 0.0)
    out_ref[share:] = jnp.where(row == 0, high.astype(F32), low).astype(BF16)


def add_packed(mine_ref, other_ref):
    total = mine_ref[...].astype(F32) + other_ref[...].astype(F32)
    share = total.shape[0] - 16
    return total[:share], total[share : share + 1] + total[share + 1 : share + 2]


def repack_kernel(mine_ref, other_ref, out_ref):
    pack_terms(out_ref, *add_packed(mine_ref, other_ref))


def unpack_kernel(mine_ref, other_ref, out_ref):
    weight_term, bias_term = add_packed(mine_ref, other_ref)
    share = weight_term.shape[0]
    out_ref[:share] = weight_term
    out_ref[share:] = jnp.broadcast_to(bias_term, (8, bias_term.shape[1]))


def keep_kernel(rep_ref, near_t_ref, far_t_ref, back_ref, grad_ref, sums_ref, near_ref, far_ref, term_ref):
    share = term_ref.shape[0] - 16
    sums = sums_ref[...]
    mine = jnp.where(rep_ref[0, 0] == 0, sums[:, :share], sums[:, share:])
    high, low = split(mine)
    grad = grad_ref[...]
    rows = ((0,), (0,))
    own = jnp.sum(grad[: grad.shape[0] // 2].astype(F32), axis=0, keepdims=True)
    pack_terms(term_ref, dot(high, grad, rows) + dot(low, grad, rows), own)
    wide = near_ref.shape[0]
    far_ref[...] = dot(far_t_ref[:wide], back_ref[...])
    near_ref[...] = dot(near_t_ref[:wide], back_ref[...])


def final_kernel(rep_ref, mine_ref, other_ref, weight_ref, bias_ref, *, scale):
    share = weight_ref.shape[0] // 2
    mine, other = mine_ref[...] * scale, other_ref[...] * scale
    first = rep_ref[0, 0] == 0
    weight_ref[:share] = jnp.where(first, mine[:share], other[:share])
    weight_ref[share:] = jnp.where(first, other[:share], mine[:share])
    bias_ref[...] = mine[share : share + 1] + other[share : share + 1]


def on_chip(kernel, shapes, scratch=(), scalars=0):
    vmem = pl.BlockSpec(memory_space=pltpu.VMEM)
    smem = pl.BlockSpec(memory_space=pltpu.SMEM)

    def call(*operands):
        return pl.pallas_call(
            kernel,
            out_shape=tuple(jax.ShapeDtypeStruct(*shape) for shape in shapes),
            in_specs=[smem] * scalars + [vmem] * (len(operands) - scalars),
            out_specs=(vmem,) * len(shapes),
            scratch_shapes=list(scratch),
            compiler_params=pltpu.CompilerParams(vmem_limit_bytes=40 << 20),
        )(*operands)

    return call


def tile_loop(target, source, partner, tiles, totals, right_of, product_of, place_of):
    slots = tiles.shape[1]

    def one(number, totals):
        k, s = number // slots, number % slots
        product = product_of(tiles[partner[k], s], right_of(k, s))
        product = product * (target[k, s] >= 0).astype(F32)
        start = place_of(k, s)
        earlier = lax.dynamic_slice_in_dim(totals, start, product.shape[0], 0)
        return lax.dynamic_update_slice_in_dim(totals, earlier + product, start, 0)

    return lax.fori_loop(0, target.shape[0] * slots, one, totals)


def slot_targets(tile_place, tile_count, partner, rep, per_side):
    places = tile_place[0, 0][partner]
    target = places // per_side
    target = jnp.bitwise_xor(target // per_side, rep) * per_side + target % per_side
    slots = places.shape[1]
    live = jnp.arange(slots, dtype=jnp.int32)[None, :] < tile_count[0, 0][partner][:, None]
    return jnp.where(live, target, -1), places % per_side


def plus(*parts):
    total = None
    for part, start, size in parts:
        rows = part[start : start + size].astype(F32)
        total = rows if total is None else total + rows
    return total


def after(value, *others):
    return lax.optimization_barrier((value, others))[0]


def dense_body(node_features, weight, bias_vector, tile_values, tile_place, tile_count, cotangent):
    loop_size = lax.axis_size("loop")
    position = lax.axis_index("loop").astype(jnp.int32)
    rep = lax.axis_index("rep").astype(jnp.int32)
    rows_own, width_in = node_features.shape
    width_out = weight.shape[1]
    _, _, partners, slots, tile, _ = tile_values.shape
    share = width_in // 2
    scale_factor = float(rows_own * loop_size * 2) ** (-0.5)
    wide, deep, rows = partners // 2 * tile, slots * 2 * tile, 2 * tile

    def move(value, masks):
        return exchange(value, masks, loop_size, 2)

    first, second = (1, 2), (2, 1)
    masks = [partner_masks([4, first[core], second[core], 8]) for core in range(2)]
    position, rep = position.reshape(1, 1), rep.reshape(1, 1)

    own_near = jnp.concatenate([node_features, move(node_features, (4, 4))], axis=0)
    own_far = [move(node_features, (z, z)) for z in (8, 12)]
    own_far = jnp.concatenate(own_far, axis=0)
    own_near = jnp.concatenate([own_near, move(own_near, first)], axis=0)
    come_near = move(own_near, second)
    own_far = jnp.concatenate([own_far, move(own_far, first)], axis=0)
    come_far = move(own_far, second)
    pair_cotangent = swap_rep(cotangent, 1, 2)

    sums, far, near_t, far_t, panel, weight, bias = on_chip(
        partial(near_kernel, masks=masks),
        [
            ((rows, width_in), F32),
            ((deep, wide), BF16),
            ((wide, deep), BF16),
            ((wide, deep), BF16),
            ((rows, width_out), BF16),
            ((width_in, width_out), BF16),
            ((1, width_out), F32),
        ],
        [pltpu.VMEM((deep, wide), BF16)],
        4,
    )(
        position, rep, tile_place[0, 0], tile_count[0], tile_values[0, 0], own_near, come_near,
        cotangent, pair_cotangent, weight, bias_vector.reshape(1, width_out),
    )
    (sums,) = on_chip(far_kernel, [((rows, width_in), F32)])(sums, far, own_far, come_far)
    far_message, output, back, grad_pre, sums = on_chip(
        middle_kernel,
        [
            ((wide // 2, width_in), BF16),
            ((rows_own, width_out), BF16),
            ((slots * rows, width_in), BF16),
            ((rows, width_out), BF16),
            ((rows, width_in), F32),
        ],
    )(sums, swap_rep(sums, 1, 2), weight, bias, panel, far_t)
    (near_message,) = on_chip(message_kernel, [((wide // 2, width_in), BF16)])(near_t, back)
    near_keep, far_keep, term = on_chip(
        keep_kernel,
        [((wide // 2, width_in), F32), ((wide // 2, width_in), F32), ((share + 16, width_out), BF16)],
        (),
        1,
    )(rep, near_t, far_t, back, grad_pre, sums)

    far_1 = move(far_message, second)
    near_1 = move(near_message, second)
    half, one = wide // 4, rows_own
    (term,) = on_chip(repack_kernel, [(term.shape, BF16)])(term, move(term, (4, 8)))
    far_2 = move(plus((far_keep, half, half), (far_1, half, half)).astype(BF16), first)
    near_2 = move(plus((near_keep, half, half), (near_1, half, half)).astype(BF16), first)
    term = after(term, far_1)
    (term,) = on_chip(repack_kernel, [(term.shape, BF16)])(term, move(term, (8, 4)))
    far_parts = (far_keep, far_1, far_2)
    near_parts = (near_keep, near_1, near_2)
    from_8 = move(plus(*((part, 0, one) for part in far_parts)).astype(BF16), (8, 8))
    from_12 = move(plus(*((part, one, one) for part in far_parts)).astype(BF16), (12, 12))
    from_4 = move(plus(*((part, one, one) for part in near_parts)).astype(BF16), (4, 4))
    term = after(term, near_1)
    (term,) = on_chip(repack_kernel, [(term.shape, BF16)])(term, move(term, (1, 2)))
    term = after(term, far_2, near_2)
    (term,) = on_chip(unpack_kernel, [((share + 8, width_out), F32)])(term, move(term, (2, 1)))
    near_parts = near_parts + (from_8, from_12, from_4)
    grad_features = plus(*((part, 0, one) for part in near_parts)).astype(BF16)

    grad_weight, grad_bias = on_chip(
        partial(final_kernel, scale=scale_factor),
        [((width_in, width_out), F32), ((1, width_out), F32)],
        (),
        1,
    )(rep, term, swap_rep(term, 1, 2))
    return (output, grad_features, grad_weight, grad_bias.reshape(width_out))


def general_body(node_features, weight, bias_vector, tile_values, tile_place, tile_count, cotangent):
    loop_size = lax.axis_size("loop")
    rep_size = lax.axis_size("rep")
    position = lax.axis_index("loop").astype(jnp.int32)
    rep = lax.axis_index("rep").astype(jnp.int32)
    rows_own, width_in = node_features.shape
    width_out = weight.shape[1]
    partners, tile = tile_values.shape[2], tile_values.shape[4]
    per_side = rows_own // tile
    panel = rep_size * per_side
    order = axis_order(loop_size)
    half = partners // 2
    share = width_in // rep_size
    scale_factor = float(rows_own * loop_size * rep_size) ** (-0.5)
    tiles = tile_values[0, 0]
    rep_bits = [1 << bit for bit in range(rep_size.bit_length() - 1)]
    partner = jnp.bitwise_xor(position, jnp.array(partner_masks(order), jnp.int32))
    target, source = slot_targets(tile_place, tile_count, partner, rep, per_side)

    def move(value, bit):
        return exchange(value, (bit, bit), loop_size, rep_size)

    gathered = node_features
    for bit in order:
        gathered = jnp.concatenate([gathered, move(gathered, bit)], axis=0)
    cotangent_rows = cotangent
    for bit in rep_bits:
        cotangent_rows = jnp.concatenate(
            [cotangent_rows, swap_rep(cotangent_rows, bit, rep_size)], axis=0
        )
    sums = tile_loop(
        target, source, partner, tiles, jnp.zeros((panel * tile, width_in), F32),
        lambda k, s: lax.dynamic_slice_in_dim(
            gathered, k * rows_own + source[k, s] * tile, tile, 0
        ),
        dot,
        lambda k, s: jnp.maximum(target[k, s], 0) * tile,
    )
    for bit in rep_bits:
        other = swap_rep(sums, bit, rep_size)
        blocks = other.reshape(rep_size, rows_own, width_in)
        blocks = jnp.stack([blocks[t ^ bit] for t in range(rep_size)])
        sums = sums + blocks.reshape(sums.shape)
    high = lax.reduce_precision(sums, 8, 7)
    low = (sums - high).astype(BF16)
    high = high.astype(BF16)
    preact = dot(high, weight) + dot(low, weight) + bias_vector[None, :]
    negative = jnp.minimum(preact, 0.0)
    own = preact[:rows_own]
    output = jnp.where(own > 0, own, jnp.expm1(negative[:rows_own])).astype(BF16)
    slope = jnp.where(preact > 0, 1.0, jnp.exp(negative))
    grad_pre = (cotangent_rows.astype(F32) * slope).astype(BF16)
    back = dot(grad_pre, weight, ((1,), (1,))).astype(BF16)
    start = rep * share
    term = dot(lax.dynamic_slice_in_dim(high, start, share, 1), grad_pre, ((0,), (0,)))
    term = term + dot(lax.dynamic_slice_in_dim(low, start, share, 1), grad_pre, ((0,), (0,)))
    bias_term = jnp.sum(grad_pre[:rows_own].astype(F32), axis=0, keepdims=True)
    term = jnp.concatenate([term, jnp.broadcast_to(bias_term, (8, width_out))], axis=0)
    adjoint = tile_loop(
        target, source, partner, tiles, jnp.zeros((partners * rows_own, width_in), F32),
        lambda k, s: lax.dynamic_slice_in_dim(back, jnp.maximum(target[k, s], 0) * tile, tile, 0),
        lambda left, right: dot(left, right, ((0,), (0,))),
        lambda k, s: k * rows_own + source[k, s] * tile,
    )
    size = half * rows_own
    for bit in order[::-1]:
        term = term + move(term, bit)
        adjoint = adjoint[:size] + move(adjoint[size:].astype(BF16), bit).astype(F32)
        size = size // 2
    shares = term[None] * scale_factor
    for bit in rep_bits:
        shares = jnp.concatenate([shares, swap_rep(shares, bit, rep_size)], axis=0)
    shares = shares[jnp.bitwise_xor(jnp.arange(rep_size, dtype=jnp.int32), rep)]
    grad_weight = shares[:, :share].reshape(width_in, width_out)
    return (output, adjoint.astype(BF16), grad_weight, jnp.sum(shares[:, share], axis=0))


def body(*arrays):
    rows_own, tile_values = arrays[0].shape[0], arrays[3]
    _, _, partners, slots, tile, _ = tile_values.shape
    groups = (lax.axis_size("rep"), partners, slots, rows_own // tile)
    return (dense_body if groups == (2, 16, 2, 1) else general_body)(*arrays)


def solution(mesh):
    return jax.shard_map(
        body,
        mesh=mesh,
        in_specs=(
            P(("loop", "rep"), None),
            P(),
            P(),
            P("loop", "rep", None, None, None, None),
            P("loop", "rep", None, None),
            P("loop", "rep", None),
            P(("loop", "rep"), None),
        ),
        out_specs=(P(("loop", "rep"), None), P(("loop", "rep"), None), P(), P()),
        check_vma=False,
    )
```

```python
from functools import partial

import jax
import jax.numpy as jnp
from jax import lax
from jax.experimental import pallas as pl
from jax.experimental.pallas import tpu as pltpu
from jax.sharding import PartitionSpec as P

BF16 = jnp.bfloat16
F32 = jnp.float32


def dot(left, right, contract=((1,), (0,))):
    return lax.dot_general(left, right, (contract, ((), ())), preferred_element_type=F32)


def axis_order(loop_size):
    bits = [1 << b for b in range(loop_size.bit_length() - 1)]
    low, high = bits[: len(bits) // 2], bits[len(bits) // 2 :]
    return high[::-1] + low


def exchange(value, masks, loop_size, rep_size):
    pairs = []
    for place in range(loop_size):
        for rep in range(rep_size):
            partner = place ^ masks[rep % 2]
            pairs.append((place * rep_size + rep, partner * rep_size + rep))
    return lax.ppermute(value, ("loop", "rep"), pairs)


def swap_rep(value, mask, rep_size):
    return lax.ppermute(value, "rep", [(r, r ^ mask) for r in range(rep_size)])


def partner_masks(order):
    masks = [0]
    for bit in order:
        masks = masks + [m ^ bit for m in masks]
    return masks


def scatter_tiles(position_ref, rep_ref, place_ref, count_ref, masks, tiles_ref, k, out, out_t, first):
    slots, tile = tiles_ref.shape[1], tiles_ref.shape[2]
    panel = out_t.shape[1] // (slots * tile)
    rep = rep_ref[0, 0]
    mask = jnp.where(rep == 0, masks[0][k], masks[1][k])
    source = jnp.bitwise_xor(position_ref[0, 0], mask)
    count = count_ref[0, source]
    cols = pl.ds((k - first) * tile, tile)
    for s in range(slots):
        one = tiles_ref[source, s]
        one_t = one.T
        row = jnp.where(s < count, jnp.bitwise_xor(place_ref[source, s], rep), -1)
        for t in range(panel):
            keep = (row == t).astype(BF16)
            rows = pl.ds((s * panel + t) * tile, tile)
            out[rows, cols] = one * keep
            out_t[cols, rows] = one_t * keep


def fold(both):
    half = both.shape[0] // 2
    return both[:half] + both[half:]


def near_kernel(
    position_ref, rep_ref, place_ref, count_ref, tiles_ref, own_ref, come_ref, far_own_ref,
    cotangent_ref, pair_ref, weight_ref, bias_ref,
    sums_ref, far_ref, near_t_ref, far_t_ref, panel_ref, weight_out_ref, bias_out_ref, near_ref, *, masks,
):
    lists = (position_ref, rep_ref, place_ref, count_ref, masks, tiles_ref)
    partners = tiles_ref.shape[0]
    half = partners // 2
    for k in range(half):
        scatter_tiles(*lists, k, near_ref, near_t_ref, 0)
    for k in range(half, partners):
        scatter_tiles(*lists, k, far_ref, far_t_ref, half)
    wide = own_ref.shape[0]
    both = dot(near_ref[:, :wide], own_ref[...]) + dot(near_ref[:, wide:], come_ref[...])
    sums_ref[...] = fold(both + dot(far_ref[:, :wide], far_own_ref[...]))
    rows = cotangent_ref.shape[0]
    panel_ref[:rows] = cotangent_ref[...]
    panel_ref[rows:] = pair_ref[...]
    weight_out_ref[...] = weight_ref[...]
    bias_out_ref[...] = bias_ref[...]


def far_kernel(sums_ref, far_ref, come_ref, out_ref):
    wide = come_ref.shape[0]
    out_ref[...] = sums_ref[...] + fold(dot(far_ref[:, wide:], come_ref[...]))


def split(value):
    high = value.astype(BF16)
    return high, (value - high.astype(F32)).astype(BF16)


def exp_less_one(value, grown):
    series = value * (1.0 + value * (1 / 2 + value * (1 / 6 + value * (1 / 24))))
    return jnp.where(value > -0.0625, series, grown - 1.0)


def middle_kernel(
    mine_ref, other_ref, weight_ref, bias_ref, panel_ref, far_t_ref,
    message_ref, output_ref, back_ref, grad_ref, sums_ref,
):
    rows = output_ref.shape[0]
    sums_ref[:rows] = mine_ref[:rows] + other_ref[rows:]
    sums_ref[rows:] = mine_ref[rows:] + other_ref[:rows]
    high, low = split(sums_ref[...])
    weight = weight_ref[...]
    preact = dot(high, weight) + dot(low, weight) + bias_ref[...]
    negative = jnp.minimum(preact, 0.0)
    grown = jnp.exp(negative)
    slope = jnp.where(preact > 0, 1.0, grown)
    own = preact[:rows]
    below = exp_less_one(negative[:rows], grown[:rows])
    output_ref[...] = jnp.where(own > 0, own, below).astype(BF16)
    grad_ref[...] = (panel_ref[...].astype(F32) * slope).astype(BF16)
    back = dot(grad_ref[...], weight, ((1,), (1,))).astype(BF16)
    back_ref[: 2 * rows] = back
    back_ref[2 * rows :] = back
    wide = message_ref.shape[0]
    message_ref[...] = dot(far_t_ref[wide:], back_ref[...]).astype(BF16)


def message_kernel(near_t_ref, back_ref, message_ref):
    wide = message_ref.shape[0]
    message_ref[...] = dot(near_t_ref[wide:], back_ref[...]).astype(BF16)


def pack_terms(out_ref, weight_term, bias_term):
    share = weight_term.shape[0]
    out_ref[:share] = weight_term.astype(BF16)
    high, low = split(bias_term)
    row = lax.broadcasted_iota(jnp.int32, (16, bias_term.shape[1]), 0)
    low = jnp.where(row == 1, low.astype(F32), 0.0)
    out_ref[share:] = jnp.where(row == 0, high.astype(F32), low).astype(BF16)


def add_packed(mine_ref, other_ref):
    total = mine_ref[...].astype(F32) + other_ref[...].astype(F32)
    share = total.shape[0] - 16
    return total[:share], total[share : share + 1] + total[share + 1 : share + 2]


def repack_kernel(mine_ref, other_ref, out_ref):
    pack_terms(out_ref, *add_packed(mine_ref, other_ref))


def unpack_kernel(mine_ref, other_ref, out_ref):
    weight_term, bias_term = add_packed(mine_ref, other_ref)
    share = weight_term.shape[0]
    out_ref[:share] = weight_term
    out_ref[share:] = jnp.broadcast_to(bias_term, (8, bias_term.shape[1]))


def keep_kernel(rep_ref, near_t_ref, far_t_ref, back_ref, grad_ref, sums_ref, near_ref, far_ref, term_ref):
    share = term_ref.shape[0] - 16
    sums = sums_ref[...]
    mine = jnp.where(rep_ref[0, 0] == 0, sums[:, :share], sums[:, share:])
    high, low = split(mine)
    grad = grad_ref[...]
    rows = ((0,), (0,))
    own = jnp.sum(grad[: grad.shape[0] // 2].astype(F32), axis=0, keepdims=True)
    pack_terms(term_ref, dot(high, grad, rows) + dot(low, grad, rows), own)
    wide = near_ref.shape[0]
    far_ref[...] = dot(far_t_ref[:wide], back_ref[...])
    near_ref[...] = dot(near_t_ref[:wide], back_ref[...])


def final_kernel(rep_ref, mine_ref, other_ref, weight_ref, bias_ref, *, scale):
    share = weight_ref.shape[0] // 2
    mine, other = mine_ref[...] * scale, other_ref[...] * scale
    first = rep_ref[0, 0] == 0
    weight_ref[:share] = jnp.where(first, mine[:share], other[:share])
    weight_ref[share:] = jnp.where(first, other[:share], mine[:share])
    bias_ref[...] = mine[share : share + 1] + other[share : share + 1]


def on_chip(kernel, shapes, scratch=(), scalars=0):
    vmem = pl.BlockSpec(memory_space=pltpu.VMEM)
    smem = pl.BlockSpec(memory_space=pltpu.SMEM)

    def call(*operands):
        return pl.pallas_call(
            kernel,
            out_shape=tuple(jax.ShapeDtypeStruct(*shape) for shape in shapes),
            in_specs=[smem] * scalars + [vmem] * (len(operands) - scalars),
            out_specs=(vmem,) * len(shapes),
            scratch_shapes=list(scratch),
            compiler_params=pltpu.CompilerParams(vmem_limit_bytes=40 << 20),
        )(*operands)

    return call


def tile_loop(target, source, partner, tiles, totals, right_of, product_of, place_of):
    slots = tiles.shape[1]

    def one(number, totals):
        k, s = number // slots, number % slots
        product = product_of(tiles[partner[k], s], right_of(k, s))
        product = product * (target[k, s] >= 0).astype(F32)
        start = place_of(k, s)
        earlier = lax.dynamic_slice_in_dim(totals, start, product.shape[0], 0)
        return lax.dynamic_update_slice_in_dim(totals, earlier + product, start, 0)

    return lax.fori_loop(0, target.shape[0] * slots, one, totals)


def slot_targets(tile_place, tile_count, partner, rep, per_side):
    places = tile_place[0, 0][partner]
    target = places // per_side
    target = jnp.bitwise_xor(target // per_side, rep) * per_side + target % per_side
    slots = places.shape[1]
    live = jnp.arange(slots, dtype=jnp.int32)[None, :] < tile_count[0, 0][partner][:, None]
    return jnp.where(live, target, -1), places % per_side


def plus(*parts):
    total = None
    for part, start, size in parts:
        rows = part[start : start + size].astype(F32)
        total = rows if total is None else total + rows
    return total


def after(value, *others):
    return lax.optimization_barrier((value, others))[0]


def dense_body(node_features, weight, bias_vector, tile_values, tile_place, tile_count, cotangent):
    loop_size = lax.axis_size("loop")
    position = lax.axis_index("loop").astype(jnp.int32)
    rep = lax.axis_index("rep").astype(jnp.int32)
    rows_own, width_in = node_features.shape
    width_out = weight.shape[1]
    _, _, partners, slots, tile, _ = tile_values.shape
    share = width_in // 2
    scale_factor = float(rows_own * loop_size * 2) ** (-0.5)
    wide, deep, rows = partners // 2 * tile, slots * 2 * tile, 2 * tile

    def move(value, masks):
        return exchange(value, masks, loop_size, 2)

    first, second = (1, 2), (2, 1)
    masks = [partner_masks([4, first[core], second[core], 8]) for core in range(2)]
    position, rep = position.reshape(1, 1), rep.reshape(1, 1)

    own_near = jnp.concatenate([node_features, move(node_features, (4, 4))], axis=0)
    own_far = [after(move(node_features, (z, z)), own_near) for z in (8, 12)]
    own_far = jnp.concatenate(own_far, axis=0)
    come = after(move(own_near, first), own_far)
    own_near = jnp.concatenate([own_near, come], axis=0)
    come_near = move(own_near, second)
    own_far = jnp.concatenate([own_far, move(own_far, first)], axis=0)
    come_far = move(own_far, second)
    pair_cotangent = swap_rep(cotangent, 1, 2)

    sums, far, near_t, far_t, panel, weight, bias = on_chip(
        partial(near_kernel, masks=masks),
        [
            ((rows, width_in), F32),
            ((deep, wide), BF16),
            ((wide, deep), BF16),
            ((wide, deep), BF16),
            ((rows, width_out), BF16),
            ((width_in, width_out), BF16),
            ((1, width_out), F32),
        ],
        [pltpu.VMEM((deep, wide), BF16)],
        4,
    )(
        position, rep, tile_place[0, 0], tile_count[0], tile_values[0, 0], own_near, come_near, own_far,
        cotangent, pair_cotangent, weight, bias_vector.reshape(1, width_out),
    )
    (sums,) = on_chip(far_kernel, [((rows, width_in), F32)])(sums, far, come_far)
    far_message, output, back, grad_pre, sums = on_chip(
        middle_kernel,
        [
            ((wide // 2, width_in), BF16),
            ((rows_own, width_out), BF16),
            ((slots * rows, width_in), BF16),
            ((rows, width_out), BF16),
            ((rows, width_in), F32),
        ],
    )(sums, swap_rep(sums, 1, 2), weight, bias, panel, far_t)
    (near_message,) = on_chip(message_kernel, [((wide // 2, width_in), BF16)])(near_t, back)
    near_keep, far_keep, term = on_chip(
        keep_kernel,
        [((wide // 2, width_in), F32), ((wide // 2, width_in), F32), ((share + 16, width_out), BF16)],
        (),
        1,
    )(rep, near_t, far_t, back, grad_pre, sums)

    far_1 = move(far_message, second)
    near_1 = move(near_message, second)
    half, one = wide // 4, rows_own
    (term,) = on_chip(repack_kernel, [(term.shape, BF16)])(term, move(term, (4, 8)))
    far_2 = move(plus((far_keep, half, half), (far_1, half, half)).astype(BF16), first)
    near_2 = move(plus((near_keep, half, half), (near_1, half, half)).astype(BF16), first)
    term = after(term, far_1)
    (term,) = on_chip(repack_kernel, [(term.shape, BF16)])(term, move(term, (8, 4)))
    far_parts = (far_keep, far_1, far_2)
    near_parts = (near_keep, near_1, near_2)
    from_8 = move(plus(*((part, 0, one) for part in far_parts)).astype(BF16), (8, 8))
    from_12 = move(plus(*((part, one, one) for part in far_parts)).astype(BF16), (12, 12))
    from_4 = move(plus(*((part, one, one) for part in near_parts)).astype(BF16), (4, 4))
    term = after(term, near_1)
    (term,) = on_chip(repack_kernel, [(term.shape, BF16)])(term, move(term, (1, 2)))
    term = after(term, far_2, near_2)
    (term,) = on_chip(unpack_kernel, [((share + 8, width_out), F32)])(term, move(term, (2, 1)))
    near_parts = near_parts + (from_8, from_12, from_4)
    grad_features = plus(*((part, 0, one) for part in near_parts)).astype(BF16)

    grad_weight, grad_bias = on_chip(
        partial(final_kernel, scale=scale_factor),
        [((width_in, width_out), F32), ((1, width_out), F32)],
        (),
        1,
    )(rep, term, swap_rep(term, 1, 2))
    return (output, grad_features, grad_weight, grad_bias.reshape(width_out))


def general_body(node_features, weight, bias_vector, tile_values, tile_place, tile_count, cotangent):
    loop_size = lax.axis_size("loop")
    rep_size = lax.axis_size("rep")
    position = lax.axis_index("loop").astype(jnp.int32)
    rep = lax.axis_index("rep").astype(jnp.int32)
    rows_own, width_in = node_features.shape
    width_out = weight.shape[1]
    partners, tile = tile_values.shape[2], tile_values.shape[4]
    per_side = rows_own // tile
    panel = rep_size * per_side
    order = axis_order(loop_size)
    half = partners // 2
    share = width_in // rep_size
    scale_factor = float(rows_own * loop_size * rep_size) ** (-0.5)
    tiles = tile_values[0, 0]
    rep_bits = [1 << bit for bit in range(rep_size.bit_length() - 1)]
    partner = jnp.bitwise_xor(position, jnp.array(partner_masks(order), jnp.int32))
    target, source = slot_targets(tile_place, tile_count, partner, rep, per_side)

    def move(value, bit):
        return exchange(value, (bit, bit), loop_size, rep_size)

    gathered = node_features
    for bit in order:
        gathered = jnp.concatenate([gathered, move(gathered, bit)], axis=0)
    cotangent_rows = cotangent
    for bit in rep_bits:
        cotangent_rows = jnp.concatenate(
            [cotangent_rows, swap_rep(cotangent_rows, bit, rep_size)], axis=0
        )
    sums = tile_loop(
        target, source, partner, tiles, jnp.zeros((panel * tile, width_in), F32),
        lambda k, s: lax.dynamic_slice_in_dim(
            gathered, k * rows_own + source[k, s] * tile, tile, 0
        ),
        dot,
        lambda k, s: jnp.maximum(target[k, s], 0) * tile,
    )
    for bit in rep_bits:
        other = swap_rep(sums, bit, rep_size)
        blocks = other.reshape(rep_size, rows_own, width_in)
        blocks = jnp.stack([blocks[t ^ bit] for t in range(rep_size)])
        sums = sums + blocks.reshape(sums.shape)
    high = lax.reduce_precision(sums, 8, 7)
    low = (sums - high).astype(BF16)
    high = high.astype(BF16)
    preact = dot(high, weight) + dot(low, weight) + bias_vector[None, :]
    negative = jnp.minimum(preact, 0.0)
    own = preact[:rows_own]
    output = jnp.where(own > 0, own, jnp.expm1(negative[:rows_own])).astype(BF16)
    slope = jnp.where(preact > 0, 1.0, jnp.exp(negative))
    grad_pre = (cotangent_rows.astype(F32) * slope).astype(BF16)
    back = dot(grad_pre, weight, ((1,), (1,))).astype(BF16)
    start = rep * share
    term = dot(lax.dynamic_slice_in_dim(high, start, share, 1), grad_pre, ((0,), (0,)))
    term = term + dot(lax.dynamic_slice_in_dim(low, start, share, 1), grad_pre, ((0,), (0,)))
    bias_term = jnp.sum(grad_pre[:rows_own].astype(F32), axis=0, keepdims=True)
    term = jnp.concatenate([term, jnp.broadcast_to(bias_term, (8, width_out))], axis=0)
    adjoint = tile_loop(
        target, source, partner, tiles, jnp.zeros((partners * rows_own, width_in), F32),
        lambda k, s: lax.dynamic_slice_in_dim(back, jnp.maximum(target[k, s], 0) * tile, tile, 0),
        lambda left, right: dot(left, right, ((0,), (0,))),
        lambda k, s: k * rows_own + source[k, s] * tile,
    )
    size = half * rows_own
    for bit in order[::-1]:
        term = term + move(term, bit)
        adjoint = adjoint[:size] + move(adjoint[size:].astype(BF16), bit).astype(F32)
        size = size // 2
    shares = term[None] * scale_factor
    for bit in rep_bits:
        shares = jnp.concatenate([shares, swap_rep(shares, bit, rep_size)], axis=0)
    shares = shares[jnp.bitwise_xor(jnp.arange(rep_size, dtype=jnp.int32), rep)]
    grad_weight = shares[:, :share].reshape(width_in, width_out)
    return (output, adjoint.astype(BF16), grad_weight, jnp.sum(shares[:, share], axis=0))


def body(*arrays):
    rows_own, tile_values = arrays[0].shape[0], arrays[3]
    _, _, partners, slots, tile, _ = tile_values.shape
    groups = (lax.axis_size("rep"), partners, slots, rows_own // tile)
    return (dense_body if groups == (2, 16, 2, 1) else general_body)(*arrays)


def solution(mesh):
    return jax.shard_map(
        body,
        mesh=mesh,
        in_specs=(
            P(("loop", "rep"), None),
            P(),
            P(),
            P("loop", "rep", None, None, None, None),
            P("loop", "rep", None, None),
            P("loop", "rep", None),
            P(("loop", "rep"), None),
        ),
        out_specs=(P(("loop", "rep"), None), P(("loop", "rep"), None), P(), P()),
        check_vma=False,
    )
```

```python
from functools import partial

import jax
import jax.numpy as jnp
from jax import lax
from jax.experimental import pallas as pl
from jax.experimental.pallas import tpu as pltpu
from jax.sharding import PartitionSpec as P

BF16 = jnp.bfloat16
F32 = jnp.float32


def dot(left, right, contract=((1,), (0,))):
    return lax.dot_general(left, right, (contract, ((), ())), preferred_element_type=F32)


def axis_order(loop_size):
    bits = [1 << b for b in range(loop_size.bit_length() - 1)]
    low, high = bits[: len(bits) // 2], bits[len(bits) // 2 :]
    return high[::-1] + low


def exchange(value, masks, loop_size, rep_size):
    pairs = []
    for place in range(loop_size):
        for rep in range(rep_size):
            partner = place ^ masks[rep % 2]
            pairs.append((place * rep_size + rep, partner * rep_size + rep))
    return lax.ppermute(value, ("loop", "rep"), pairs)


def swap_rep(value, mask, rep_size):
    return lax.ppermute(value, "rep", [(r, r ^ mask) for r in range(rep_size)])


def partner_masks(order):
    masks = [0]
    for bit in order:
        masks = masks + [m ^ bit for m in masks]
    return masks


def scatter_tiles(position_ref, rep_ref, place_ref, count_ref, masks, tiles_ref, k, out, out_t, first):
    slots, tile = tiles_ref.shape[1], tiles_ref.shape[2]
    panel = out_t.shape[1] // (slots * tile)
    rep = rep_ref[0, 0]
    mask = jnp.where(rep == 0, masks[0][k], masks[1][k])
    source = jnp.bitwise_xor(position_ref[0, 0], mask)
    count = count_ref[0, source]
    cols = pl.ds((k - first) * tile, tile)
    for s in range(slots):
        one = tiles_ref[source, s]
        one_t = one.T
        row = jnp.where(s < count, jnp.bitwise_xor(place_ref[source, s], rep), -1)
        for t in range(panel):
            keep = (row == t).astype(BF16)
            rows = pl.ds((s * panel + t) * tile, tile)
            out[rows, cols] = one * keep
            out_t[cols, rows] = one_t * keep


def fold(both):
    half = both.shape[0] // 2
    return both[:half] + both[half:]


def near_kernel(
    position_ref, rep_ref, place_ref, count_ref, tiles_ref, own_ref, come_ref, far_own_ref,
    cotangent_ref, pair_ref, weight_ref, bias_ref,
    sums_ref, far_ref, near_t_ref, far_t_ref, panel_ref, weight_out_ref, bias_out_ref, near_ref, *, masks,
):
    lists = (position_ref, rep_ref, place_ref, count_ref, masks, tiles_ref)
    partners = tiles_ref.shape[0]
    half = partners // 2
    for k in range(half):
        scatter_tiles(*lists, k, near_ref, near_t_ref, 0)
    for k in range(half, partners):
        scatter_tiles(*lists, k, far_ref, far_t_ref, half)
    wide = own_ref.shape[0]
    both = dot(near_ref[:, :wide], own_ref[...]) + dot(near_ref[:, wide:], come_ref[...])
    sums_ref[...] = fold(both + dot(far_ref[:, :wide], far_own_ref[...]))
    rows = cotangent_ref.shape[0]
    panel_ref[:rows] = cotangent_ref[...]
    panel_ref[rows:] = pair_ref[...]
    weight_out_ref[...] = weight_ref[...]
    bias_out_ref[...] = bias_ref[...]


def far_kernel(sums_ref, far_ref, come_ref, out_ref):
    wide = come_ref.shape[0]
    out_ref[...] = sums_ref[...] + fold(dot(far_ref[:, wide:], come_ref[...]))


def split(value):
    high = value.astype(BF16)
    return high, (value - high.astype(F32)).astype(BF16)


def exp_less_one(value, grown):
    series = value * (1.0 + value * (1 / 2 + value * (1 / 6 + value * (1 / 24))))
    return jnp.where(value > -0.0625, series, grown - 1.0)


def middle_kernel(
    mine_ref, other_ref, weight_ref, bias_ref, panel_ref, far_t_ref,
    message_ref, preact_ref, back_ref, grad_ref, sums_ref,
):
    rows = preact_ref.shape[0]
    sums_ref[:rows] = mine_ref[:rows] + other_ref[rows:]
    sums_ref[rows:] = mine_ref[rows:] + other_ref[:rows]
    high, low = split(sums_ref[...])
    weight = weight_ref[...]
    preact = dot(high, weight) + dot(low, weight) + bias_ref[...]
    negative = jnp.minimum(preact, 0.0)
    slope = jnp.where(preact > 0, 1.0, jnp.exp(negative))
    preact_ref[...] = preact[:rows]
    grad_ref[...] = (panel_ref[...].astype(F32) * slope).astype(BF16)
    back = dot(grad_ref[...], weight, ((1,), (1,))).astype(BF16)
    back_ref[: 2 * rows] = back
    back_ref[2 * rows :] = back
    wide = message_ref.shape[0]
    message_ref[...] = dot(far_t_ref[wide:], back_ref[...]).astype(BF16)


def message_kernel(near_t_ref, back_ref, message_ref):
    wide = message_ref.shape[0]
    message_ref[...] = dot(near_t_ref[wide:], back_ref[...]).astype(BF16)


def pack_terms(out_ref, weight_term, bias_term):
    share = weight_term.shape[0]
    out_ref[:share] = weight_term.astype(BF16)
    high, low = split(bias_term)
    row = lax.broadcasted_iota(jnp.int32, (16, bias_term.shape[1]), 0)
    low = jnp.where(row == 1, low.astype(F32), 0.0)
    out_ref[share:] = jnp.where(row == 0, high.astype(F32), low).astype(BF16)


def add_packed(mine_ref, other_ref):
    total = mine_ref[...].astype(F32) + other_ref[...].astype(F32)
    share = total.shape[0] - 16
    return total[:share], total[share : share + 1] + total[share + 1 : share + 2]


def repack_kernel(mine_ref, other_ref, out_ref):
    pack_terms(out_ref, *add_packed(mine_ref, other_ref))


def unpack_kernel(mine_ref, other_ref, out_ref):
    weight_term, bias_term = add_packed(mine_ref, other_ref)
    share = weight_term.shape[0]
    out_ref[:share] = weight_term
    out_ref[share:] = jnp.broadcast_to(bias_term, (8, bias_term.shape[1]))


def term_kernel(rep_ref, grad_ref, sums_ref, term_ref):
    share = term_ref.shape[0] - 16
    sums = sums_ref[...]
    mine = jnp.where(rep_ref[0, 0] == 0, sums[:, :share], sums[:, share:])
    high, low = split(mine)
    grad = grad_ref[...]
    rows = ((0,), (0,))
    own = jnp.sum(grad[: grad.shape[0] // 2].astype(F32), axis=0, keepdims=True)
    pack_terms(term_ref, dot(high, grad, rows) + dot(low, grad, rows), own)


def keep_kernel(near_t_ref, far_t_ref, back_ref, preact_ref, near_ref, far_ref, output_ref):
    wide = near_ref.shape[0]
    far_ref[...] = dot(far_t_ref[:wide], back_ref[...])
    near_ref[...] = dot(near_t_ref[:wide], back_ref[...])
    own = preact_ref[...]
    negative = jnp.minimum(own, 0.0)
    below = exp_less_one(negative, jnp.exp(negative))
    output_ref[...] = jnp.where(own > 0, own, below).astype(BF16)


def final_kernel(rep_ref, mine_ref, other_ref, weight_ref, bias_ref, *, scale):
    share = weight_ref.shape[0] // 2
    mine, other = mine_ref[...] * scale, other_ref[...] * scale
    first = rep_ref[0, 0] == 0
    weight_ref[:share] = jnp.where(first, mine[:share], other[:share])
    weight_ref[share:] = jnp.where(first, other[:share], mine[:share])
    bias_ref[...] = mine[share : share + 1] + other[share : share + 1]


def on_chip(kernel, shapes, scratch=(), scalars=0):
    vmem = pl.BlockSpec(memory_space=pltpu.VMEM)
    smem = pl.BlockSpec(memory_space=pltpu.SMEM)

    def call(*operands):
        return pl.pallas_call(
            kernel,
            out_shape=tuple(jax.ShapeDtypeStruct(*shape) for shape in shapes),
            in_specs=[smem] * scalars + [vmem] * (len(operands) - scalars),
            out_specs=(vmem,) * len(shapes),
            scratch_shapes=list(scratch),
            compiler_params=pltpu.CompilerParams(vmem_limit_bytes=40 << 20),
        )(*operands)

    return call


def tile_loop(target, source, partner, tiles, totals, right_of, product_of, place_of):
    slots = tiles.shape[1]

    def one(number, totals):
        k, s = number // slots, number % slots
        product = product_of(tiles[partner[k], s], right_of(k, s))
        product = product * (target[k, s] >= 0).astype(F32)
        start = place_of(k, s)
        earlier = lax.dynamic_slice_in_dim(totals, start, product.shape[0], 0)
        return lax.dynamic_update_slice_in_dim(totals, earlier + product, start, 0)

    return lax.fori_loop(0, target.shape[0] * slots, one, totals)


def slot_targets(tile_place, tile_count, partner, rep, per_side):
    places = tile_place[0, 0][partner]
    target = places // per_side
    target = jnp.bitwise_xor(target // per_side, rep) * per_side + target % per_side
    slots = places.shape[1]
    live = jnp.arange(slots, dtype=jnp.int32)[None, :] < tile_count[0, 0][partner][:, None]
    return jnp.where(live, target, -1), places % per_side


def plus(*parts):
    total = None
    for part, start, size in parts:
        rows = part[start : start + size].astype(F32)
        total = rows if total is None else total + rows
    return total


def after(value, *others):
    return lax.optimization_barrier((value, others))[0]


def dense_body(node_features, weight, bias_vector, tile_values, tile_place, tile_count, cotangent):
    loop_size = lax.axis_size("loop")
    position = lax.axis_index("loop").astype(jnp.int32)
    rep = lax.axis_index("rep").astype(jnp.int32)
    rows_own, width_in = node_features.shape
    width_out = weight.shape[1]
    _, _, partners, slots, tile, _ = tile_values.shape
    share = width_in // 2
    scale_factor = float(rows_own * loop_size * 2) ** (-0.5)
    wide, deep, rows = partners // 2 * tile, slots * 2 * tile, 2 * tile

    def move(value, masks):
        return exchange(value, masks, loop_size, 2)

    first, second = (1, 2), (2, 1)
    masks = [partner_masks([4, first[core], second[core], 8]) for core in range(2)]
    position, rep = position.reshape(1, 1), rep.reshape(1, 1)

    own_near = jnp.concatenate([node_features, move(node_features, (4, 4))], axis=0)
    own_far = [after(move(node_features, (z, z)), own_near) for z in (8, 12)]
    own_far = jnp.concatenate(own_far, axis=0)
    come = after(move(own_near, first), own_far)
    own_near = jnp.concatenate([own_near, come], axis=0)
    come_near = move(own_near, second)
    own_far = jnp.concatenate([own_far, move(own_far, first)], axis=0)
    come_far = move(own_far, second)
    pair_cotangent = swap_rep(cotangent, 1, 2)

    sums, far, near_t, far_t, panel, weight, bias = on_chip(
        partial(near_kernel, masks=masks),
        [
            ((rows, width_in), F32),
            ((deep, wide), BF16),
            ((wide, deep), BF16),
            ((wide, deep), BF16),
            ((rows, width_out), BF16),
            ((width_in, width_out), BF16),
            ((1, width_out), F32),
        ],
        [pltpu.VMEM((deep, wide), BF16)],
        4,
    )(
        position, rep, tile_place[0, 0], tile_count[0], tile_values[0, 0], own_near, come_near, own_far,
        cotangent, pair_cotangent, weight, bias_vector.reshape(1, width_out),
    )
    (sums,) = on_chip(far_kernel, [((rows, width_in), F32)])(sums, far, come_far)
    far_message, preact, back, grad_pre, sums = on_chip(
        middle_kernel,
        [
            ((wide // 2, width_in), BF16),
            ((rows_own, width_out), F32),
            ((slots * rows, width_in), BF16),
            ((rows, width_out), BF16),
            ((rows, width_in), F32),
        ],
    )(sums, swap_rep(sums, 1, 2), weight, bias, panel, far_t)
    (near_message,) = on_chip(message_kernel, [((wide // 2, width_in), BF16)])(near_t, back)
    (term,) = on_chip(term_kernel, [((share + 16, width_out), BF16)], (), 1)(rep, grad_pre, sums)
    near_keep, far_keep, output = on_chip(
        keep_kernel,
        [((wide // 2, width_in), F32), ((wide // 2, width_in), F32), ((rows_own, width_out), BF16)],
    )(near_t, far_t, back, preact)

    far_1 = move(far_message, second)
    near_1 = move(near_message, second)
    half, one = wide // 4, rows_own
    (term,) = on_chip(repack_kernel, [(term.shape, BF16)])(term, move(term, (4, 8)))
    far_2 = move(plus((far_keep, half, half), (far_1, half, half)).astype(BF16), first)
    near_2 = move(plus((near_keep, half, half), (near_1, half, half)).astype(BF16), first)
    term = after(term, far_1)
    (term,) = on_chip(repack_kernel, [(term.shape, BF16)])(term, move(term, (8, 4)))
    far_parts = (far_keep, far_1, far_2)
    near_parts = (near_keep, near_1, near_2)
    from_8 = move(plus(*((part, 0, one) for part in far_parts)).astype(BF16), (8, 8))
    from_12 = move(plus(*((part, one, one) for part in far_parts)).astype(BF16), (12, 12))
    from_4 = move(plus(*((part, one, one) for part in near_parts)).astype(BF16), (4, 4))
    term = after(term, near_1)
    (term,) = on_chip(repack_kernel, [(term.shape, BF16)])(term, move(term, (1, 2)))
    term = after(term, far_2, near_2)
    (term,) = on_chip(unpack_kernel, [((share + 8, width_out), F32)])(term, move(term, (2, 1)))
    near_parts = near_parts + (from_8, from_12, from_4)
    grad_features = plus(*((part, 0, one) for part in near_parts)).astype(BF16)

    grad_weight, grad_bias = on_chip(
        partial(final_kernel, scale=scale_factor),
        [((width_in, width_out), F32), ((1, width_out), F32)],
        (),
        1,
    )(rep, term, swap_rep(term, 1, 2))
    return (output, grad_features, grad_weight, grad_bias.reshape(width_out))


def general_body(node_features, weight, bias_vector, tile_values, tile_place, tile_count, cotangent):
    loop_size = lax.axis_size("loop")
    rep_size = lax.axis_size("rep")
    position = lax.axis_index("loop").astype(jnp.int32)
    rep = lax.axis_index("rep").astype(jnp.int32)
    rows_own, width_in = node_features.shape
    width_out = weight.shape[1]
    partners, tile = tile_values.shape[2], tile_values.shape[4]
    per_side = rows_own // tile
    panel = rep_size * per_side
    order = axis_order(loop_size)
    half = partners // 2
    share = width_in // rep_size
    scale_factor = float(rows_own * loop_size * rep_size) ** (-0.5)
    tiles = tile_values[0, 0]
    rep_bits = [1 << bit for bit in range(rep_size.bit_length() - 1)]
    partner = jnp.bitwise_xor(position, jnp.array(partner_masks(order), jnp.int32))
    target, source = slot_targets(tile_place, tile_count, partner, rep, per_side)

    def move(value, bit):
        return exchange(value, (bit, bit), loop_size, rep_size)

    gathered = node_features
    for bit in order:
        gathered = jnp.concatenate([gathered, move(gathered, bit)], axis=0)
    cotangent_rows = cotangent
    for bit in rep_bits:
        cotangent_rows = jnp.concatenate(
            [cotangent_rows, swap_rep(cotangent_rows, bit, rep_size)], axis=0
        )
    sums = tile_loop(
        target, source, partner, tiles, jnp.zeros((panel * tile, width_in), F32),
        lambda k, s: lax.dynamic_slice_in_dim(
            gathered, k * rows_own + source[k, s] * tile, tile, 0
        ),
        dot,
        lambda k, s: jnp.maximum(target[k, s], 0) * tile,
    )
    for bit in rep_bits:
        other = swap_rep(sums, bit, rep_size)
        blocks = other.reshape(rep_size, rows_own, width_in)
        blocks = jnp.stack([blocks[t ^ bit] for t in range(rep_size)])
        sums = sums + blocks.reshape(sums.shape)
    high = lax.reduce_precision(sums, 8, 7)
    low = (sums - high).astype(BF16)
    high = high.astype(BF16)
    preact = dot(high, weight) + dot(low, weight) + bias_vector[None, :]
    negative = jnp.minimum(preact, 0.0)
    own = preact[:rows_own]
    output = jnp.where(own > 0, own, jnp.expm1(negative[:rows_own])).astype(BF16)
    slope = jnp.where(preact > 0, 1.0, jnp.exp(negative))
    grad_pre = (cotangent_rows.astype(F32) * slope).astype(BF16)
    back = dot(grad_pre, weight, ((1,), (1,))).astype(BF16)
    start = rep * share
    term = dot(lax.dynamic_slice_in_dim(high, start, share, 1), grad_pre, ((0,), (0,)))
    term = term + dot(lax.dynamic_slice_in_dim(low, start, share, 1), grad_pre, ((0,), (0,)))
    bias_term = jnp.sum(grad_pre[:rows_own].astype(F32), axis=0, keepdims=True)
    term = jnp.concatenate([term, jnp.broadcast_to(bias_term, (8, width_out))], axis=0)
    adjoint = tile_loop(
        target, source, partner, tiles, jnp.zeros((partners * rows_own, width_in), F32),
        lambda k, s: lax.dynamic_slice_in_dim(back, jnp.maximum(target[k, s], 0) * tile, tile, 0),
        lambda left, right: dot(left, right, ((0,), (0,))),
        lambda k, s: k * rows_own + source[k, s] * tile,
    )
    size = half * rows_own
    for bit in order[::-1]:
        term = term + move(term, bit)
        adjoint = adjoint[:size] + move(adjoint[size:].astype(BF16), bit).astype(F32)
        size = size // 2
    shares = term[None] * scale_factor
    for bit in rep_bits:
        shares = jnp.concatenate([shares, swap_rep(shares, bit, rep_size)], axis=0)
    shares = shares[jnp.bitwise_xor(jnp.arange(rep_size, dtype=jnp.int32), rep)]
    grad_weight = shares[:, :share].reshape(width_in, width_out)
    return (output, adjoint.astype(BF16), grad_weight, jnp.sum(shares[:, share], axis=0))


def body(*arrays):
    rows_own, tile_values = arrays[0].shape[0], arrays[3]
    _, _, partners, slots, tile, _ = tile_values.shape
    groups = (lax.axis_size("rep"), partners, slots, rows_own // tile)
    return (dense_body if groups == (2, 16, 2, 1) else general_body)(*arrays)


def solution(mesh):
    return jax.shard_map(
        body,
        mesh=mesh,
        in_specs=(
            P(("loop", "rep"), None),
            P(),
            P(),
            P("loop", "rep", None, None, None, None),
            P("loop", "rep", None, None),
            P("loop", "rep", None),
            P(("loop", "rep"), None),
        ),
        out_specs=(P(("loop", "rep"), None), P(("loop", "rep"), None), P(), P()),
        check_vma=False,
    )
```

```python
from functools import partial

import jax
import jax.numpy as jnp
from jax import lax
from jax.experimental import pallas as pl
from jax.experimental.pallas import tpu as pltpu
from jax.sharding import PartitionSpec as P

BF16 = jnp.bfloat16
F32 = jnp.float32


def dot(left, right, contract=((1,), (0,))):
    return lax.dot_general(left, right, (contract, ((), ())), preferred_element_type=F32)


def axis_order(loop_size):
    bits = [1 << b for b in range(loop_size.bit_length() - 1)]
    low, high = bits[: len(bits) // 2], bits[len(bits) // 2 :]
    return high[::-1] + low


def exchange(value, masks, loop_size, rep_size):
    pairs = []
    for place in range(loop_size):
        for rep in range(rep_size):
            partner = place ^ masks[rep % 2]
            pairs.append((place * rep_size + rep, partner * rep_size + rep))
    return lax.ppermute(value, ("loop", "rep"), pairs)


def swap_rep(value, mask, rep_size):
    return lax.ppermute(value, "rep", [(r, r ^ mask) for r in range(rep_size)])


def partner_masks(order):
    masks = [0]
    for bit in order:
        masks = masks + [m ^ bit for m in masks]
    return masks


def scatter_tiles(position_ref, rep_ref, place_ref, count_ref, masks, tiles_ref, k, out, out_t, first):
    slots, tile = tiles_ref.shape[1], tiles_ref.shape[2]
    panel = out_t.shape[1] // (slots * tile)
    rep = rep_ref[0, 0]
    mask = jnp.where(rep == 0, masks[0][k], masks[1][k])
    source = jnp.bitwise_xor(position_ref[0, 0], mask)
    count = count_ref[0, source]
    cols = pl.ds((k - first) * tile, tile)
    for s in range(slots):
        one = tiles_ref[source, s]
        one_t = one.T
        row = jnp.where(s < count, jnp.bitwise_xor(place_ref[source, s], rep), -1)
        for t in range(panel):
            keep = (row == t).astype(BF16)
            rows = pl.ds((s * panel + t) * tile, tile)
            out[rows, cols] = one * keep
            out_t[cols, rows] = one_t * keep


def fold(both):
    half = both.shape[0] // 2
    return both[:half] + both[half:]


def near_kernel(
    position_ref, rep_ref, place_ref, count_ref, tiles_ref, own_ref, come_ref, far_own_ref,
    cotangent_ref, pair_ref, weight_ref, bias_ref,
    sums_ref, far_ref, near_t_ref, far_t_ref, panel_ref, weight_out_ref, bias_out_ref, near_ref, *, masks,
):
    lists = (position_ref, rep_ref, place_ref, count_ref, masks, tiles_ref)
    partners = tiles_ref.shape[0]
    half = partners // 2
    for k in range(half):
        scatter_tiles(*lists, k, near_ref, near_t_ref, 0)
    for k in range(half, partners):
        scatter_tiles(*lists, k, far_ref, far_t_ref, half)
    wide = own_ref.shape[0]
    both = dot(near_ref[:, :wide], own_ref[...]) + dot(near_ref[:, wide:], come_ref[...])
    sums_ref[...] = fold(both + dot(far_ref[:, :wide], far_own_ref[...]))
    rows = cotangent_ref.shape[0]
    panel_ref[:rows] = cotangent_ref[...]
    panel_ref[rows:] = pair_ref[...]
    weight_out_ref[...] = weight_ref[...]
    bias_out_ref[...] = bias_ref[...]


def far_kernel(sums_ref, far_ref, come_ref, out_ref, last_ref):
    wide = come_ref.shape[0]
    last = fold(dot(far_ref[:, wide:], come_ref[...]))
    out_ref[...] = sums_ref[...] + last
    last_ref[...] = last.astype(BF16)


def split(value):
    high = value.astype(BF16)
    return high, (value - high.astype(F32)).astype(BF16)


def exp_less_one(value, grown):
    series = value * (1.0 + value * (1 / 2 + value * (1 / 6 + value * (1 / 24))))
    return jnp.where(value > -0.0625, series, grown - 1.0)


def middle_kernel(
    mine_ref, early_ref, last_ref, weight_ref, bias_ref, panel_ref, far_t_ref,
    message_ref, preact_ref, back_ref, grad_ref, sums_ref,
):
    rows = preact_ref.shape[0]
    other = early_ref[...] + last_ref[...].astype(F32)
    sums_ref[:rows] = mine_ref[:rows] + other[rows:]
    sums_ref[rows:] = mine_ref[rows:] + other[:rows]
    high, low = split(sums_ref[...])
    weight = weight_ref[...]
    preact = dot(high, weight) + dot(low, weight) + bias_ref[...]
    negative = jnp.minimum(preact, 0.0)
    slope = jnp.where(preact > 0, 1.0, jnp.exp(negative))
    preact_ref[...] = preact[:rows]
    grad_ref[...] = (panel_ref[...].astype(F32) * slope).astype(BF16)
    back = dot(grad_ref[...], weight, ((1,), (1,))).astype(BF16)
    back_ref[: 2 * rows] = back
    back_ref[2 * rows :] = back
    wide = message_ref.shape[0]
    message_ref[...] = dot(far_t_ref[wide:], back_ref[...]).astype(BF16)


def message_kernel(near_t_ref, back_ref, message_ref):
    wide = message_ref.shape[0]
    message_ref[...] = dot(near_t_ref[wide:], back_ref[...]).astype(BF16)


def pack_terms(out_ref, weight_term, bias_term):
    share = weight_term.shape[0]
    out_ref[:share] = weight_term.astype(BF16)
    high, low = split(bias_term)
    row = lax.broadcasted_iota(jnp.int32, (16, bias_term.shape[1]), 0)
    low = jnp.where(row == 1, low.astype(F32), 0.0)
    out_ref[share:] = jnp.where(row == 0, high.astype(F32), low).astype(BF16)


def add_packed(mine_ref, other_ref):
    total = mine_ref[...].astype(F32) + other_ref[...].astype(F32)
    share = total.shape[0] - 16
    return total[:share], total[share : share + 1] + total[share + 1 : share + 2]


def repack_kernel(mine_ref, other_ref, out_ref):
    pack_terms(out_ref, *add_packed(mine_ref, other_ref))


def unpack_kernel(mine_ref, other_ref, out_ref):
    weight_term, bias_term = add_packed(mine_ref, other_ref)
    share = weight_term.shape[0]
    out_ref[:share] = weight_term
    out_ref[share:] = jnp.broadcast_to(bias_term, (8, bias_term.shape[1]))


def term_kernel(rep_ref, grad_ref, sums_ref, term_ref):
    share = term_ref.shape[0] - 16
    sums = sums_ref[...]
    mine = jnp.where(rep_ref[0, 0] == 0, sums[:, :share], sums[:, share:])
    high, low = split(mine)
    grad = grad_ref[...]
    rows = ((0,), (0,))
    own = jnp.sum(grad[: grad.shape[0] // 2].astype(F32), axis=0, keepdims=True)
    pack_terms(term_ref, dot(high, grad, rows) + dot(low, grad, rows), own)


def keep_kernel(near_t_ref, far_t_ref, back_ref, preact_ref, near_ref, far_ref, output_ref):
    wide = near_ref.shape[0]
    far_ref[...] = dot(far_t_ref[:wide], back_ref[...])
    near_ref[...] = dot(near_t_ref[:wide], back_ref[...])
    own = preact_ref[...]
    negative = jnp.minimum(own, 0.0)
    below = exp_less_one(negative, jnp.exp(negative))
    output_ref[...] = jnp.where(own > 0, own, below).astype(BF16)


def final_kernel(rep_ref, mine_ref, other_ref, weight_ref, bias_ref, *, scale):
    share = weight_ref.shape[0] // 2
    mine, other = mine_ref[...] * scale, other_ref[...] * scale
    first = rep_ref[0, 0] == 0
    weight_ref[:share] = jnp.where(first, mine[:share], other[:share])
    weight_ref[share:] = jnp.where(first, other[:share], mine[:share])
    bias_ref[...] = mine[share : share + 1] + other[share : share + 1]


def on_chip(kernel, shapes, scratch=(), scalars=0):
    vmem = pl.BlockSpec(memory_space=pltpu.VMEM)
    smem = pl.BlockSpec(memory_space=pltpu.SMEM)

    def call(*operands):
        return pl.pallas_call(
            kernel,
            out_shape=tuple(jax.ShapeDtypeStruct(*shape) for shape in shapes),
            in_specs=[smem] * scalars + [vmem] * (len(operands) - scalars),
            out_specs=(vmem,) * len(shapes),
            scratch_shapes=list(scratch),
            compiler_params=pltpu.CompilerParams(vmem_limit_bytes=40 << 20),
        )(*operands)

    return call


def tile_loop(target, source, partner, tiles, totals, right_of, product_of, place_of):
    slots = tiles.shape[1]

    def one(number, totals):
        k, s = number // slots, number % slots
        product = product_of(tiles[partner[k], s], right_of(k, s))
        product = product * (target[k, s] >= 0).astype(F32)
        start = place_of(k, s)
        earlier = lax.dynamic_slice_in_dim(totals, start, product.shape[0], 0)
        return lax.dynamic_update_slice_in_dim(totals, earlier + product, start, 0)

    return lax.fori_loop(0, target.shape[0] * slots, one, totals)


def slot_targets(tile_place, tile_count, partner, rep, per_side):
    places = tile_place[0, 0][partner]
    target = places // per_side
    target = jnp.bitwise_xor(target // per_side, rep) * per_side + target % per_side
    slots = places.shape[1]
    live = jnp.arange(slots, dtype=jnp.int32)[None, :] < tile_count[0, 0][partner][:, None]
    return jnp.where(live, target, -1), places % per_side


def plus(*parts):
    total = None
    for part, start, size in parts:
        rows = part[start : start + size].astype(F32)
        total = rows if total is None else total + rows
    return total


def after(value, *others):
    return lax.optimization_barrier((value, others))[0]


def dense_body(node_features, weight, bias_vector, tile_values, tile_place, tile_count, cotangent):
    loop_size = lax.axis_size("loop")
    position = lax.axis_index("loop").astype(jnp.int32)
    rep = lax.axis_index("rep").astype(jnp.int32)
    rows_own, width_in = node_features.shape
    width_out = weight.shape[1]
    _, _, partners, slots, tile, _ = tile_values.shape
    share = width_in // 2
    scale_factor = float(rows_own * loop_size * 2) ** (-0.5)
    wide, deep, rows = partners // 2 * tile, slots * 2 * tile, 2 * tile

    def move(value, masks):
        return exchange(value, masks, loop_size, 2)

    first, second = (1, 2), (2, 1)
    masks = [partner_masks([4, first[core], second[core], 8]) for core in range(2)]
    position, rep = position.reshape(1, 1), rep.reshape(1, 1)

    own_near = jnp.concatenate([node_features, move(node_features, (4, 4))], axis=0)
    own_far = [after(move(node_features, (z, z)), own_near) for z in (8, 12)]
    own_far = jnp.concatenate(own_far, axis=0)
    come = after(move(own_near, first), own_far)
    own_near = jnp.concatenate([own_near, come], axis=0)
    come_near = move(own_near, second)
    own_far = jnp.concatenate([own_far, move(own_far, first)], axis=0)
    come_far = move(own_far, second)
    pair_cotangent = swap_rep(cotangent, 1, 2)

    sums, far, near_t, far_t, panel, weight, bias = on_chip(
        partial(near_kernel, masks=masks),
        [
            ((rows, width_in), F32),
            ((deep, wide), BF16),
            ((wide, deep), BF16),
            ((wide, deep), BF16),
            ((rows, width_out), BF16),
            ((width_in, width_out), BF16),
            ((1, width_out), F32),
        ],
        [pltpu.VMEM((deep, wide), BF16)],
        4,
    )(
        position, rep, tile_place[0, 0], tile_count[0], tile_values[0, 0], own_near, come_near, own_far,
        cotangent, pair_cotangent, weight, bias_vector.reshape(1, width_out),
    )
    early = swap_rep(sums, 1, 2)
    sums, last = on_chip(far_kernel, [((rows, width_in), F32), ((rows, width_in), BF16)])(sums, far, come_far)
    far_message, preact, back, grad_pre, sums = on_chip(
        middle_kernel,
        [
            ((wide // 2, width_in), BF16),
            ((rows_own, width_out), F32),
            ((slots * rows, width_in), BF16),
            ((rows, width_out), BF16),
            ((rows, width_in), F32),
        ],
    )(sums, early, swap_rep(last, 1, 2), weight, bias, panel, far_t)
    (near_message,) = on_chip(message_kernel, [((wide // 2, width_in), BF16)])(near_t, back)
    (term,) = on_chip(term_kernel, [((share + 16, width_out), BF16)], (), 1)(rep, grad_pre, sums)
    near_keep, far_keep, output = on_chip(
        keep_kernel,
        [((wide // 2, width_in), F32), ((wide // 2, width_in), F32), ((rows_own, width_out), BF16)],
    )(near_t, far_t, back, preact)

    far_1 = move(far_message, second)
    near_1 = move(near_message, second)
    half, one = wide // 4, rows_own
    (term,) = on_chip(repack_kernel, [(term.shape, BF16)])(term, move(term, (4, 8)))
    far_2 = move(plus((far_keep, half, half), (far_1, half, half)).astype(BF16), first)
    near_2 = move(plus((near_keep, half, half), (near_1, half, half)).astype(BF16), first)
    term = after(term, far_1)
    (term,) = on_chip(repack_kernel, [(term.shape, BF16)])(term, move(term, (8, 4)))
    far_parts = (far_keep, far_1, far_2)
    near_parts = (near_keep, near_1, near_2)
    from_8 = move(plus(*((part, 0, one) for part in far_parts)).astype(BF16), (8, 8))
    from_12 = move(plus(*((part, one, one) for part in far_parts)).astype(BF16), (12, 12))
    from_4 = move(plus(*((part, one, one) for part in near_parts)).astype(BF16), (4, 4))
    term = after(term, near_1)
    (term,) = on_chip(repack_kernel, [(term.shape, BF16)])(term, move(term, (1, 2)))
    term = after(term, far_2, near_2)
    (term,) = on_chip(unpack_kernel, [((share + 8, width_out), F32)])(term, move(term, (2, 1)))
    near_parts = near_parts + (from_8, from_12, from_4)
    grad_features = plus(*((part, 0, one) for part in near_parts)).astype(BF16)

    grad_weight, grad_bias = on_chip(
        partial(final_kernel, scale=scale_factor),
        [((width_in, width_out), F32), ((1, width_out), F32)],
        (),
        1,
    )(rep, term, swap_rep(term, 1, 2))
    return (output, grad_features, grad_weight, grad_bias.reshape(width_out))


def general_body(node_features, weight, bias_vector, tile_values, tile_place, tile_count, cotangent):
    loop_size = lax.axis_size("loop")
    rep_size = lax.axis_size("rep")
    position = lax.axis_index("loop").astype(jnp.int32)
    rep = lax.axis_index("rep").astype(jnp.int32)
    rows_own, width_in = node_features.shape
    width_out = weight.shape[1]
    partners, tile = tile_values.shape[2], tile_values.shape[4]
    per_side = rows_own // tile
    panel = rep_size * per_side
    order = axis_order(loop_size)
    half = partners // 2
    share = width_in // rep_size
    scale_factor = float(rows_own * loop_size * rep_size) ** (-0.5)
    tiles = tile_values[0, 0]
    rep_bits = [1 << bit for bit in range(rep_size.bit_length() - 1)]
    partner = jnp.bitwise_xor(position, jnp.array(partner_masks(order), jnp.int32))
    target, source = slot_targets(tile_place, tile_count, partner, rep, per_side)

    def move(value, bit):
        return exchange(value, (bit, bit), loop_size, rep_size)

    gathered = node_features
    for bit in order:
        gathered = jnp.concatenate([gathered, move(gathered, bit)], axis=0)
    cotangent_rows = cotangent
    for bit in rep_bits:
        cotangent_rows = jnp.concatenate(
            [cotangent_rows, swap_rep(cotangent_rows, bit, rep_size)], axis=0
        )
    sums = tile_loop(
        target, source, partner, tiles, jnp.zeros((panel * tile, width_in), F32),
        lambda k, s: lax.dynamic_slice_in_dim(
            gathered, k * rows_own + source[k, s] * tile, tile, 0
        ),
        dot,
        lambda k, s: jnp.maximum(target[k, s], 0) * tile,
    )
    for bit in rep_bits:
        other = swap_rep(sums, bit, rep_size)
        blocks = other.reshape(rep_size, rows_own, width_in)
        blocks = jnp.stack([blocks[t ^ bit] for t in range(rep_size)])
        sums = sums + blocks.reshape(sums.shape)
    high = lax.reduce_precision(sums, 8, 7)
    low = (sums - high).astype(BF16)
    high = high.astype(BF16)
    preact = dot(high, weight) + dot(low, weight) + bias_vector[None, :]
    negative = jnp.minimum(preact, 0.0)
    own = preact[:rows_own]
    output = jnp.where(own > 0, own, jnp.expm1(negative[:rows_own])).astype(BF16)
    slope = jnp.where(preact > 0, 1.0, jnp.exp(negative))
    grad_pre = (cotangent_rows.astype(F32) * slope).astype(BF16)
    back = dot(grad_pre, weight, ((1,), (1,))).astype(BF16)
    start = rep * share
    term = dot(lax.dynamic_slice_in_dim(high, start, share, 1), grad_pre, ((0,), (0,)))
    term = term + dot(lax.dynamic_slice_in_dim(low, start, share, 1), grad_pre, ((0,), (0,)))
    bias_term = jnp.sum(grad_pre[:rows_own].astype(F32), axis=0, keepdims=True)
    term = jnp.concatenate([term, jnp.broadcast_to(bias_term, (8, width_out))], axis=0)
    adjoint = tile_loop(
        target, source, partner, tiles, jnp.zeros((partners * rows_own, width_in), F32),
        lambda k, s: lax.dynamic_slice_in_dim(back, jnp.maximum(target[k, s], 0) * tile, tile, 0),
        lambda left, right: dot(left, right, ((0,), (0,))),
        lambda k, s: k * rows_own + source[k, s] * tile,
    )
    size = half * rows_own
    for bit in order[::-1]:
        term = term + move(term, bit)
        adjoint = adjoint[:size] + move(adjoint[size:].astype(BF16), bit).astype(F32)
        size = size // 2
    shares = term[None] * scale_factor
    for bit in rep_bits:
        shares = jnp.concatenate([shares, swap_rep(shares, bit, rep_size)], axis=0)
    shares = shares[jnp.bitwise_xor(jnp.arange(rep_size, dtype=jnp.int32), rep)]
    grad_weight = shares[:, :share].reshape(width_in, width_out)
    return (output, adjoint.astype(BF16), grad_weight, jnp.sum(shares[:, share], axis=0))


def body(*arrays):
    rows_own, tile_values = arrays[0].shape[0], arrays[3]
    _, _, partners, slots, tile, _ = tile_values.shape
    groups = (lax.axis_size("rep"), partners, slots, rows_own // tile)
    return (dense_body if groups == (2, 16, 2, 1) else general_body)(*arrays)


def solution(mesh):
    return jax.shard_map(
        body,
        mesh=mesh,
        in_specs=(
            P(("loop", "rep"), None),
            P(),
            P(),
            P("loop", "rep", None, None, None, None),
            P("loop", "rep", None, None),
            P("loop", "rep", None),
            P(("loop", "rep"), None),
        ),
        out_specs=(P(("loop", "rep"), None), P(("loop", "rep"), None), P(), P()),
        check_vma=False,
    )
```

```python
from functools import partial

import jax
import jax.numpy as jnp
from jax import lax
from jax.experimental import pallas as pl
from jax.experimental.pallas import tpu as pltpu
from jax.sharding import PartitionSpec as P

BF16 = jnp.bfloat16
F32 = jnp.float32


def dot(left, right, contract=((1,), (0,))):
    return lax.dot_general(left, right, (contract, ((), ())), preferred_element_type=F32)


def axis_order(loop_size):
    bits = [1 << b for b in range(loop_size.bit_length() - 1)]
    low, high = bits[: len(bits) // 2], bits[len(bits) // 2 :]
    return high[::-1] + low


def exchange(value, masks, loop_size, rep_size):
    pairs = []
    for place in range(loop_size):
        for rep in range(rep_size):
            partner = place ^ masks[rep % 2]
            pairs.append((place * rep_size + rep, partner * rep_size + rep))
    return lax.ppermute(value, ("loop", "rep"), pairs)


def swap_rep(value, mask, rep_size):
    return lax.ppermute(value, "rep", [(r, r ^ mask) for r in range(rep_size)])


def partner_masks(order):
    masks = [0]
    for bit in order:
        masks = masks + [m ^ bit for m in masks]
    return masks


def scatter_tiles(position_ref, rep_ref, place_ref, count_ref, masks, tiles_ref, k, out, out_t, first):
    slots, tile = tiles_ref.shape[1], tiles_ref.shape[2]
    panel = out_t.shape[1] // (slots * tile)
    rep = rep_ref[0, 0]
    mask = jnp.where(rep == 0, masks[0][k], masks[1][k])
    source = jnp.bitwise_xor(position_ref[0, 0], mask)
    count = count_ref[0, source]
    cols = pl.ds((k - first) * tile, tile)
    for s in range(slots):
        one = tiles_ref[source, s]
        one_t = one.T
        row = jnp.where(s < count, jnp.bitwise_xor(place_ref[source, s], rep), -1)
        for t in range(panel):
            keep = (row == t).astype(BF16)
            rows = pl.ds((s * panel + t) * tile, tile)
            out[rows, cols] = one * keep
            out_t[cols, rows] = one_t * keep


def fold(both):
    half = both.shape[0] // 2
    return both[:half] + both[half:]


def near_kernel(
    position_ref, rep_ref, place_ref, count_ref, tiles_ref, own_ref, come_ref, far_own_ref,
    cotangent_ref, pair_ref, weight_ref, bias_ref,
    sums_ref, far_ref, near_t_ref, far_t_ref, panel_ref, weight_out_ref, bias_out_ref, near_ref, *, masks,
):
    lists = (position_ref, rep_ref, place_ref, count_ref, masks, tiles_ref)
    partners = tiles_ref.shape[0]
    half = partners // 2
    for k in range(half):
        scatter_tiles(*lists, k, near_ref, near_t_ref, 0)
    for k in range(half, partners):
        scatter_tiles(*lists, k, far_ref, far_t_ref, half)
    wide = own_ref.shape[0]
    both = dot(near_ref[:, :wide], own_ref[...]) + dot(near_ref[:, wide:], come_ref[...])
    sums_ref[...] = fold(both + dot(far_ref[:, :wide], far_own_ref[...]))
    rows = cotangent_ref.shape[0]
    panel_ref[:rows] = cotangent_ref[...]
    panel_ref[rows:] = pair_ref[...]
    weight_out_ref[...] = weight_ref[...]
    bias_out_ref[...] = bias_ref[...]


def far_kernel(sums_ref, far_ref, come_ref, out_ref):
    wide = come_ref.shape[0]
    out_ref[...] = sums_ref[...] + fold(dot(far_ref[:, wide:], come_ref[...]))


def split(value):
    high = value.astype(BF16)
    return high, (value - high.astype(F32)).astype(BF16)


def exp_less_one(value, grown):
    series = value * (1.0 + value * (1 / 2 + value * (1 / 6 + value * (1 / 24))))
    return jnp.where(value > -0.0625, series, grown - 1.0)


def middle_kernel(
    mine_ref, other_ref, weight_ref, bias_ref, panel_ref, far_t_ref,
    message_ref, preact_ref, back_ref, grad_ref, sums_ref,
):
    rows = preact_ref.shape[0]
    sums_ref[:rows] = mine_ref[:rows] + other_ref[rows:]
    sums_ref[rows:] = mine_ref[rows:] + other_ref[:rows]
    high, low = split(sums_ref[...])
    weight = weight_ref[...]
    preact = dot(high, weight) + dot(low, weight) + bias_ref[...]
    negative = jnp.minimum(preact, 0.0)
    slope = jnp.where(preact > 0, 1.0, jnp.exp(negative))
    preact_ref[...] = preact[:rows]
    grad_ref[...] = (panel_ref[...].astype(F32) * slope).astype(BF16)
    back = dot(grad_ref[...], weight, ((1,), (1,))).astype(BF16)
    back_ref[: 2 * rows] = back
    back_ref[2 * rows :] = back
    wide = message_ref.shape[0]
    message_ref[...] = dot(far_t_ref[wide:], back_ref[...]).astype(BF16)


def message_kernel(near_t_ref, back_ref, message_ref):
    wide = message_ref.shape[0]
    message_ref[...] = dot(near_t_ref[wide:], back_ref[...]).astype(BF16)


def pack_terms(out_ref, weight_term, bias_term):
    share = weight_term.shape[0]
    out_ref[:share] = weight_term.astype(BF16)
    high, low = split(bias_term)
    row = lax.broadcasted_iota(jnp.int32, (16, bias_term.shape[1]), 0)
    low = jnp.where(row == 1, low.astype(F32), 0.0)
    out_ref[share:] = jnp.where(row == 0, high.astype(F32), low).astype(BF16)


def add_packed(mine_ref, other_ref):
    total = mine_ref[...].astype(F32) + other_ref[...].astype(F32)
    share = total.shape[0] - 16
    return total[:share], total[share : share + 1] + total[share + 1 : share + 2]


def repack_kernel(mine_ref, other_ref, out_ref):
    pack_terms(out_ref, *add_packed(mine_ref, other_ref))


def unpack_kernel(mine_ref, other_ref, out_ref):
    weight_term, bias_term = add_packed(mine_ref, other_ref)
    share = weight_term.shape[0]
    out_ref[:share] = weight_term
    out_ref[share:] = jnp.broadcast_to(bias_term, (8, bias_term.shape[1]))


def term_kernel(rep_ref, grad_ref, sums_ref, term_ref):
    share = term_ref.shape[0] - 16
    sums = sums_ref[...]
    mine = jnp.where(rep_ref[0, 0] == 0, sums[:, :share], sums[:, share:])
    high, low = split(mine)
    grad = grad_ref[...]
    rows = ((0,), (0,))
    own = jnp.sum(grad[: grad.shape[0] // 2].astype(F32), axis=0, keepdims=True)
    pack_terms(term_ref, dot(high, grad, rows) + dot(low, grad, rows), own)


def keep_kernel(near_t_ref, far_t_ref, back_ref, preact_ref, near_ref, far_ref, output_ref):
    wide = near_ref.shape[0]
    far_ref[...] = dot(far_t_ref[:wide], back_ref[...])
    near_ref[...] = dot(near_t_ref[:wide], back_ref[...])
    own = preact_ref[...]
    negative = jnp.minimum(own, 0.0)
    below = exp_less_one(negative, jnp.exp(negative))
    output_ref[...] = jnp.where(own > 0, own, below).astype(BF16)


def final_kernel(rep_ref, mine_ref, other_ref, weight_ref, bias_ref, *, scale):
    share = weight_ref.shape[0] // 2
    mine, other = mine_ref[...] * scale, other_ref[...] * scale
    first = rep_ref[0, 0] == 0
    weight_ref[:share] = jnp.where(first, mine[:share], other[:share])
    weight_ref[share:] = jnp.where(first, other[:share], mine[:share])
    bias_ref[...] = mine[share : share + 1] + other[share : share + 1]


def on_chip(kernel, shapes, scratch=(), scalars=0):
    vmem = pl.BlockSpec(memory_space=pltpu.VMEM)
    smem = pl.BlockSpec(memory_space=pltpu.SMEM)

    def call(*operands):
        return pl.pallas_call(
            kernel,
            out_shape=tuple(jax.ShapeDtypeStruct(*shape) for shape in shapes),
            in_specs=[smem] * scalars + [vmem] * (len(operands) - scalars),
            out_specs=(vmem,) * len(shapes),
            scratch_shapes=list(scratch),
            compiler_params=pltpu.CompilerParams(vmem_limit_bytes=40 << 20),
        )(*operands)

    return call


def tile_loop(target, source, partner, tiles, totals, right_of, product_of, place_of):
    slots = tiles.shape[1]

    def one(number, totals):
        k, s = number // slots, number % slots
        product = product_of(tiles[partner[k], s], right_of(k, s))
        product = product * (target[k, s] >= 0).astype(F32)
        start = place_of(k, s)
        earlier = lax.dynamic_slice_in_dim(totals, start, product.shape[0], 0)
        return lax.dynamic_update_slice_in_dim(totals, earlier + product, start, 0)

    return lax.fori_loop(0, target.shape[0] * slots, one, totals)


def slot_targets(tile_place, tile_count, partner, rep, per_side):
    places = tile_place[0, 0][partner]
    target = places // per_side
    target = jnp.bitwise_xor(target // per_side, rep) * per_side + target % per_side
    slots = places.shape[1]
    live = jnp.arange(slots, dtype=jnp.int32)[None, :] < tile_count[0, 0][partner][:, None]
    return jnp.where(live, target, -1), places % per_side


def plus(*parts):
    total = None
    for part, start, size in parts:
        rows = part[start : start + size].astype(F32)
        total = rows if total is None else total + rows
    return total


def after(value, *others):
    return lax.optimization_barrier((value, others))[0]


def dense_body(node_features, weight, bias_vector, tile_values, tile_place, tile_count, cotangent):
    loop_size = lax.axis_size("loop")
    position = lax.axis_index("loop").astype(jnp.int32)
    rep = lax.axis_index("rep").astype(jnp.int32)
    rows_own, width_in = node_features.shape
    width_out = weight.shape[1]
    _, _, partners, slots, tile, _ = tile_values.shape
    share = width_in // 2
    scale_factor = float(rows_own * loop_size * 2) ** (-0.5)
    wide, deep, rows = partners // 2 * tile, slots * 2 * tile, 2 * tile

    def move(value, masks):
        return exchange(value, masks, loop_size, 2)

    first, second = (1, 2), (2, 1)
    masks = [partner_masks([4, first[core], second[core], 8]) for core in range(2)]
    position, rep = position.reshape(1, 1), rep.reshape(1, 1)

    own_near = jnp.concatenate([node_features, move(node_features, (4, 4))], axis=0)
    own_far = [after(move(node_features, (z, z)), own_near) for z in (12, 8)]
    own_far = jnp.concatenate(own_far[::-1], axis=0)
    come = after(move(own_near, first), own_far)
    own_near = jnp.concatenate([own_near, come], axis=0)
    come_near = move(own_near, second)
    own_far = jnp.concatenate([own_far, move(own_far, first)], axis=0)
    come_far = move(own_far, second)
    pair_cotangent = swap_rep(cotangent, 1, 2)

    sums, far, near_t, far_t, panel, weight, bias = on_chip(
        partial(near_kernel, masks=masks),
        [
            ((rows, width_in), F32),
            ((deep, wide), BF16),
            ((wide, deep), BF16),
            ((wide, deep), BF16),
            ((rows, width_out), BF16),
            ((width_in, width_out), BF16),
            ((1, width_out), F32),
        ],
        [pltpu.VMEM((deep, wide), BF16)],
        4,
    )(
        position, rep, tile_place[0, 0], tile_count[0], tile_values[0, 0], own_near, come_near, own_far,
        cotangent, pair_cotangent, weight, bias_vector.reshape(1, width_out),
    )
    (sums,) = on_chip(far_kernel, [((rows, width_in), F32)])(sums, far, come_far)
    far_message, preact, back, grad_pre, sums = on_chip(
        middle_kernel,
        [
            ((wide // 2, width_in), BF16),
            ((rows_own, width_out), F32),
            ((slots * rows, width_in), BF16),
            ((rows, width_out), BF16),
            ((rows, width_in), F32),
        ],
    )(sums, swap_rep(sums, 1, 2), weight, bias, panel, far_t)
    (near_message,) = on_chip(message_kernel, [((wide // 2, width_in), BF16)])(near_t, back)
    (term,) = on_chip(term_kernel, [((share + 16, width_out), BF16)], (), 1)(rep, grad_pre, sums)
    near_keep, far_keep, output = on_chip(
        keep_kernel,
        [((wide // 2, width_in), F32), ((wide // 2, width_in), F32), ((rows_own, width_out), BF16)],
    )(near_t, far_t, back, preact)

    far_1 = move(far_message, second)
    near_1 = move(near_message, second)
    half, one = wide // 4, rows_own
    (term,) = on_chip(repack_kernel, [(term.shape, BF16)])(term, move(term, (4, 8)))
    far_2 = move(plus((far_keep, half, half), (far_1, half, half)).astype(BF16), first)
    near_2 = move(plus((near_keep, half, half), (near_1, half, half)).astype(BF16), first)
    term = after(term, far_1)
    (term,) = on_chip(repack_kernel, [(term.shape, BF16)])(term, move(term, (8, 4)))
    far_parts = (far_keep, far_1, far_2)
    near_parts = (near_keep, near_1, near_2)
    from_8 = move(plus(*((part, 0, one) for part in far_parts)).astype(BF16), (8, 8))
    from_12 = move(plus(*((part, one, one) for part in far_parts)).astype(BF16), (12, 12))
    from_4 = move(plus(*((part, one, one) for part in near_parts)).astype(BF16), (4, 4))
    term = after(term, near_1)
    (term,) = on_chip(repack_kernel, [(term.shape, BF16)])(term, move(term, (1, 2)))
    term = after(term, far_2, near_2)
    (term,) = on_chip(unpack_kernel, [((share + 8, width_out), F32)])(term, move(term, (2, 1)))
    near_parts = near_parts + (from_8, from_12, from_4)
    grad_features = plus(*((part, 0, one) for part in near_parts)).astype(BF16)

    grad_weight, grad_bias = on_chip(
        partial(final_kernel, scale=scale_factor),
        [((width_in, width_out), F32), ((1, width_out), F32)],
        (),
        1,
    )(rep, term, swap_rep(term, 1, 2))
    return (output, grad_features, grad_weight, grad_bias.reshape(width_out))


def general_body(node_features, weight, bias_vector, tile_values, tile_place, tile_count, cotangent):
    loop_size = lax.axis_size("loop")
    rep_size = lax.axis_size("rep")
    position = lax.axis_index("loop").astype(jnp.int32)
    rep = lax.axis_index("rep").astype(jnp.int32)
    rows_own, width_in = node_features.shape
    width_out = weight.shape[1]
    partners, tile = tile_values.shape[2], tile_values.shape[4]
    per_side = rows_own // tile
    panel = rep_size * per_side
    order = axis_order(loop_size)
    half = partners // 2
    share = width_in // rep_size
    scale_factor = float(rows_own * loop_size * rep_size) ** (-0.5)
    tiles = tile_values[0, 0]
    rep_bits = [1 << bit for bit in range(rep_size.bit_length() - 1)]
    partner = jnp.bitwise_xor(position, jnp.array(partner_masks(order), jnp.int32))
    target, source = slot_targets(tile_place, tile_count, partner, rep, per_side)

    def move(value, bit):
        return exchange(value, (bit, bit), loop_size, rep_size)

    gathered = node_features
    for bit in order:
        gathered = jnp.concatenate([gathered, move(gathered, bit)], axis=0)
    cotangent_rows = cotangent
    for bit in rep_bits:
        cotangent_rows = jnp.concatenate(
            [cotangent_rows, swap_rep(cotangent_rows, bit, rep_size)], axis=0
        )
    sums = tile_loop(
        target, source, partner, tiles, jnp.zeros((panel * tile, width_in), F32),
        lambda k, s: lax.dynamic_slice_in_dim(
            gathered, k * rows_own + source[k, s] * tile, tile, 0
        ),
        dot,
        lambda k, s: jnp.maximum(target[k, s], 0) * tile,
    )
    for bit in rep_bits:
        other = swap_rep(sums, bit, rep_size)
        blocks = other.reshape(rep_size, rows_own, width_in)
        blocks = jnp.stack([blocks[t ^ bit] for t in range(rep_size)])
        sums = sums + blocks.reshape(sums.shape)
    high = lax.reduce_precision(sums, 8, 7)
    low = (sums - high).astype(BF16)
    high = high.astype(BF16)
    preact = dot(high, weight) + dot(low, weight) + bias_vector[None, :]
    negative = jnp.minimum(preact, 0.0)
    own = preact[:rows_own]
    output = jnp.where(own > 0, own, jnp.expm1(negative[:rows_own])).astype(BF16)
    slope = jnp.where(preact > 0, 1.0, jnp.exp(negative))
    grad_pre = (cotangent_rows.astype(F32) * slope).astype(BF16)
    back = dot(grad_pre, weight, ((1,), (1,))).astype(BF16)
    start = rep * share
    term = dot(lax.dynamic_slice_in_dim(high, start, share, 1), grad_pre, ((0,), (0,)))
    term = term + dot(lax.dynamic_slice_in_dim(low, start, share, 1), grad_pre, ((0,), (0,)))
    bias_term = jnp.sum(grad_pre[:rows_own].astype(F32), axis=0, keepdims=True)
    term = jnp.concatenate([term, jnp.broadcast_to(bias_term, (8, width_out))], axis=0)
    adjoint = tile_loop(
        target, source, partner, tiles, jnp.zeros((partners * rows_own, width_in), F32),
        lambda k, s: lax.dynamic_slice_in_dim(back, jnp.maximum(target[k, s], 0) * tile, tile, 0),
        lambda left, right: dot(left, right, ((0,), (0,))),
        lambda k, s: k * rows_own + source[k, s] * tile,
    )
    size = half * rows_own
    for bit in order[::-1]:
        term = term + move(term, bit)
        adjoint = adjoint[:size] + move(adjoint[size:].astype(BF16), bit).astype(F32)
        size = size // 2
    shares = term[None] * scale_factor
    for bit in rep_bits:
        shares = jnp.concatenate([shares, swap_rep(shares, bit, rep_size)], axis=0)
    shares = shares[jnp.bitwise_xor(jnp.arange(rep_size, dtype=jnp.int32), rep)]
    grad_weight = shares[:, :share].reshape(width_in, width_out)
    return (output, adjoint.astype(BF16), grad_weight, jnp.sum(shares[:, share], axis=0))


def body(*arrays):
    rows_own, tile_values = arrays[0].shape[0], arrays[3]
    _, _, partners, slots, tile, _ = tile_values.shape
    groups = (lax.axis_size("rep"), partners, slots, rows_own // tile)
    return (dense_body if groups == (2, 16, 2, 1) else general_body)(*arrays)


def solution(mesh):
    return jax.shard_map(
        body,
        mesh=mesh,
        in_specs=(
            P(("loop", "rep"), None),
            P(),
            P(),
            P("loop", "rep", None, None, None, None),
            P("loop", "rep", None, None),
            P("loop", "rep", None),
            P(("loop", "rep"), None),
        ),
        out_specs=(P(("loop", "rep"), None), P(("loop", "rep"), None), P(), P()),
        check_vma=False,
    )
```

```python
from functools import partial

import jax
import jax.numpy as jnp
from jax import lax
from jax.experimental import pallas as pl
from jax.experimental.pallas import tpu as pltpu
from jax.sharding import PartitionSpec as P

BF16 = jnp.bfloat16
F32 = jnp.float32


def dot(left, right, contract=((1,), (0,))):
    return lax.dot_general(left, right, (contract, ((), ())), preferred_element_type=F32)


def axis_order(loop_size):
    bits = [1 << b for b in range(loop_size.bit_length() - 1)]
    low, high = bits[: len(bits) // 2], bits[len(bits) // 2 :]
    return high[::-1] + low


def exchange(value, masks, loop_size, rep_size):
    pairs = []
    for place in range(loop_size):
        for rep in range(rep_size):
            partner = place ^ masks[rep % 2]
            pairs.append((place * rep_size + rep, partner * rep_size + rep))
    return lax.ppermute(value, ("loop", "rep"), pairs)


def swap_rep(value, mask, rep_size):
    return lax.ppermute(value, "rep", [(r, r ^ mask) for r in range(rep_size)])


def partner_masks(order):
    masks = [0]
    for bit in order:
        masks = masks + [m ^ bit for m in masks]
    return masks


def scatter_tiles(position_ref, rep_ref, place_ref, count_ref, masks, tiles_ref, k, out, out_t, first):
    slots, tile = tiles_ref.shape[1], tiles_ref.shape[2]
    panel = out_t.shape[1] // (slots * tile)
    rep = rep_ref[0, 0]
    mask = jnp.where(rep == 0, masks[0][k], masks[1][k])
    source = jnp.bitwise_xor(position_ref[0, 0], mask)
    count = count_ref[0, source]
    cols = pl.ds((k - first) * tile, tile)
    for s in range(slots):
        one = tiles_ref[source, s]
        one_t = one.T
        row = jnp.where(s < count, jnp.bitwise_xor(place_ref[source, s], rep), -1)
        for t in range(panel):
            keep = (row == t).astype(BF16)
            rows = pl.ds((s * panel + t) * tile, tile)
            out[rows, cols] = one * keep
            out_t[cols, rows] = one_t * keep


def fold(both):
    half = both.shape[0] // 2
    return both[:half] + both[half:]


def near_kernel(
    position_ref, rep_ref, place_ref, count_ref, tiles_ref, own_ref, come_ref, far_own_ref,
    cotangent_ref, pair_ref, weight_ref, bias_ref,
    sums_ref, far_ref, near_t_ref, far_t_ref, panel_ref, weight_out_ref, bias_out_ref, near_ref, *, masks,
):
    lists = (position_ref, rep_ref, place_ref, count_ref, masks, tiles_ref)
    partners = tiles_ref.shape[0]
    half = partners // 2
    for k in range(half):
        scatter_tiles(*lists, k, near_ref, near_t_ref, 0)
    for k in range(half, partners):
        scatter_tiles(*lists, k, far_ref, far_t_ref, half)
    wide = own_ref.shape[0]
    both = dot(near_ref[:, :wide], own_ref[...]) + dot(near_ref[:, wide:], come_ref[...])
    sums_ref[...] = fold(both + dot(far_ref[:, :wide], far_own_ref[...]))
    rows = cotangent_ref.shape[0]
    panel_ref[:rows] = cotangent_ref[...]
    panel_ref[rows:] = pair_ref[...]
    weight_out_ref[...] = weight_ref[...]
    bias_out_ref[...] = bias_ref[...]


def far_kernel(sums_ref, far_ref, come_ref, out_ref):
    wide = come_ref.shape[0]
    out_ref[...] = sums_ref[...] + fold(dot(far_ref[:, wide:], come_ref[...]))


def split(value):
    high = value.astype(BF16)
    return high, (value - high.astype(F32)).astype(BF16)


def exp_less_one(value, grown):
    series = value * (1.0 + value * (1 / 2 + value * (1 / 6 + value * (1 / 24))))
    return jnp.where(value > -0.0625, series, grown - 1.0)


def middle_kernel(
    mine_ref, other_ref, weight_ref, bias_ref, panel_ref, far_t_ref,
    message_ref, preact_ref, back_ref, grad_ref, sums_ref,
):
    rows = preact_ref.shape[0]
    sums_ref[:rows] = mine_ref[:rows] + other_ref[rows:]
    sums_ref[rows:] = mine_ref[rows:] + other_ref[:rows]
    high, low = split(sums_ref[...])
    weight = weight_ref[...]
    preact = dot(high, weight) + dot(low, weight) + bias_ref[...]
    negative = jnp.minimum(preact, 0.0)
    slope = jnp.where(preact > 0, 1.0, jnp.exp(negative))
    preact_ref[...] = preact[:rows]
    grad_ref[...] = (panel_ref[...].astype(F32) * slope).astype(BF16)
    back = dot(grad_ref[...], weight, ((1,), (1,))).astype(BF16)
    back_ref[: 2 * rows] = back
    back_ref[2 * rows :] = back
    wide = message_ref.shape[0]
    message_ref[...] = dot(far_t_ref[wide:], back_ref[...]).astype(BF16)


def message_kernel(near_t_ref, back_ref, message_ref):
    wide = message_ref.shape[0]
    message_ref[...] = dot(near_t_ref[wide:], back_ref[...]).astype(BF16)


def pack_terms(out_ref, weight_term, bias_term):
    share = weight_term.shape[0]
    out_ref[:share] = weight_term.astype(BF16)
    high, low = split(bias_term)
    row = lax.broadcasted_iota(jnp.int32, (16, bias_term.shape[1]), 0)
    low = jnp.where(row == 1, low.astype(F32), 0.0)
    out_ref[share:] = jnp.where(row == 0, high.astype(F32), low).astype(BF16)


def add_packed(mine_ref, other_ref):
    total = mine_ref[...].astype(F32) + other_ref[...].astype(F32)
    share = total.shape[0] - 16
    return total[:share], total[share : share + 1] + total[share + 1 : share + 2]


def repack_kernel(mine_ref, other_ref, out_ref):
    pack_terms(out_ref, *add_packed(mine_ref, other_ref))


def unpack_kernel(mine_ref, other_ref, out_ref):
    weight_term, bias_term = add_packed(mine_ref, other_ref)
    share = weight_term.shape[0]
    out_ref[:share] = weight_term
    out_ref[share:] = jnp.broadcast_to(bias_term, (8, bias_term.shape[1]))


def term_kernel(rep_ref, grad_ref, sums_ref, term_ref):
    share = term_ref.shape[0] - 16
    sums = sums_ref[...]
    mine = jnp.where(rep_ref[0, 0] == 0, sums[:, :share], sums[:, share:])
    high, low = split(mine)
    grad = grad_ref[...]
    rows = ((0,), (0,))
    own = jnp.sum(grad[: grad.shape[0] // 2].astype(F32), axis=0, keepdims=True)
    pack_terms(term_ref, dot(high, grad, rows) + dot(low, grad, rows), own)


def keep_kernel(near_t_ref, far_t_ref, back_ref, preact_ref, near_ref, far_ref, output_ref):
    wide = near_ref.shape[0]
    far_ref[...] = dot(far_t_ref[:wide], back_ref[...])
    near_ref[...] = dot(near_t_ref[:wide], back_ref[...])
    own = preact_ref[...]
    negative = jnp.minimum(own, 0.0)
    below = exp_less_one(negative, jnp.exp(negative))
    output_ref[...] = jnp.where(own > 0, own, below).astype(BF16)


def final_kernel(rep_ref, mine_ref, other_ref, weight_ref, bias_ref, *, scale):
    share = weight_ref.shape[0] // 2
    mine, other = mine_ref[...] * scale, other_ref[...] * scale
    first = rep_ref[0, 0] == 0
    weight_ref[:share] = jnp.where(first, mine[:share], other[:share])
    weight_ref[share:] = jnp.where(first, other[:share], mine[:share])
    bias_ref[...] = mine[share : share + 1] + other[share : share + 1]


def on_chip(kernel, shapes, scratch=(), scalars=0):
    vmem = pl.BlockSpec(memory_space=pltpu.VMEM)
    smem = pl.BlockSpec(memory_space=pltpu.SMEM)

    def call(*operands):
        return pl.pallas_call(
            kernel,
            out_shape=tuple(jax.ShapeDtypeStruct(*shape) for shape in shapes),
            in_specs=[smem] * scalars + [vmem] * (len(operands) - scalars),
            out_specs=(vmem,) * len(shapes),
            scratch_shapes=list(scratch),
            compiler_params=pltpu.CompilerParams(vmem_limit_bytes=40 << 20),
        )(*operands)

    return call


def tile_loop(target, source, partner, tiles, totals, right_of, product_of, place_of):
    slots = tiles.shape[1]

    def one(number, totals):
        k, s = number // slots, number % slots
        product = product_of(tiles[partner[k], s], right_of(k, s))
        product = product * (target[k, s] >= 0).astype(F32)
        start = place_of(k, s)
        earlier = lax.dynamic_slice_in_dim(totals, start, product.shape[0], 0)
        return lax.dynamic_update_slice_in_dim(totals, earlier + product, start, 0)

    return lax.fori_loop(0, target.shape[0] * slots, one, totals)


def slot_targets(tile_place, tile_count, partner, rep, per_side):
    places = tile_place[0, 0][partner]
    target = places // per_side
    target = jnp.bitwise_xor(target // per_side, rep) * per_side + target % per_side
    slots = places.shape[1]
    live = jnp.arange(slots, dtype=jnp.int32)[None, :] < tile_count[0, 0][partner][:, None]
    return jnp.where(live, target, -1), places % per_side


def plus(*parts):
    total = None
    for part, start, size in parts:
        rows = part[start : start + size].astype(F32)
        total = rows if total is None else total + rows
    return total


def after(value, *others):
    return lax.optimization_barrier((value, others))[0]


def dense_body(node_features, weight, bias_vector, tile_values, tile_place, tile_count, cotangent):
    loop_size = lax.axis_size("loop")
    position = lax.axis_index("loop").astype(jnp.int32)
    rep = lax.axis_index("rep").astype(jnp.int32)
    rows_own, width_in = node_features.shape
    width_out = weight.shape[1]
    _, _, partners, slots, tile, _ = tile_values.shape
    share = width_in // 2
    scale_factor = float(rows_own * loop_size * 2) ** (-0.5)
    wide, deep, rows = partners // 2 * tile, slots * 2 * tile, 2 * tile

    def move(value, masks):
        return exchange(value, masks, loop_size, 2)

    first, second = (1, 2), (2, 1)
    masks = [partner_masks([4, first[core], second[core], 8]) for core in range(2)]
    position, rep = position.reshape(1, 1), rep.reshape(1, 1)

    own_near = jnp.concatenate([node_features, move(node_features, (4, 4))], axis=0)
    own_far = [after(move(node_features, (z, z)), own_near) for z in (8, 12)]
    own_far = jnp.concatenate(own_far, axis=0)
    come = after(move(own_near, first), own_far)
    own_near = jnp.concatenate([own_near, come], axis=0)
    come_near = move(own_near, second)
    own_far = jnp.concatenate([own_far, move(own_far, first)], axis=0)
    come_far = move(own_far, second)
    pair_cotangent = swap_rep(cotangent, 1, 2)

    sums, far, near_t, far_t, panel, weight, bias = on_chip(
        partial(near_kernel, masks=masks),
        [
            ((rows, width_in), F32),
            ((deep, wide), BF16),
            ((wide, deep), BF16),
            ((wide, deep), BF16),
            ((rows, width_out), BF16),
            ((width_in, width_out), BF16),
            ((1, width_out), F32),
        ],
        [pltpu.VMEM((deep, wide), BF16)],
        4,
    )(
        position, rep, tile_place[0, 0], tile_count[0], tile_values[0, 0], own_near, come_near, own_far,
        cotangent, pair_cotangent, weight, bias_vector.reshape(1, width_out),
    )
    (sums,) = on_chip(far_kernel, [((rows, width_in), F32)])(sums, far, come_far)
    far_message, preact, back, grad_pre, sums = on_chip(
        middle_kernel,
        [
            ((wide // 2, width_in), BF16),
            ((rows_own, width_out), F32),
            ((slots * rows, width_in), BF16),
            ((rows, width_out), BF16),
            ((rows, width_in), F32),
        ],
    )(sums, swap_rep(sums, 1, 2), weight, bias, panel, far_t)
    (near_message,) = on_chip(message_kernel, [((wide // 2, width_in), BF16)])(near_t, back)
    (term,) = on_chip(term_kernel, [((share + 16, width_out), BF16)], (), 1)(rep, grad_pre, sums)
    near_keep, far_keep, output = on_chip(
        keep_kernel,
        [((wide // 2, width_in), F32), ((wide // 2, width_in), F32), ((rows_own, width_out), BF16)],
    )(near_t, far_t, back, preact)

    far_1 = move(far_message, second)
    near_1 = move(near_message, second)
    half, one = wide // 4, rows_own
    (term,) = on_chip(repack_kernel, [(term.shape, BF16)])(term, move(term, (4, 8)))
    far_2 = move(after(plus((far_keep, half, half), (far_1, half, half)).astype(BF16), term), first)
    near_2 = move(plus((near_keep, half, half), (near_1, half, half)).astype(BF16), first)
    term = after(term, far_1)
    (term,) = on_chip(repack_kernel, [(term.shape, BF16)])(term, move(term, (8, 4)))
    far_parts = (far_keep, far_1, far_2)
    near_parts = (near_keep, near_1, near_2)
    from_8 = move(plus(*((part, 0, one) for part in far_parts)).astype(BF16), (8, 8))
    from_12 = move(plus(*((part, one, one) for part in far_parts)).astype(BF16), (12, 12))
    from_4 = move(plus(*((part, one, one) for part in near_parts)).astype(BF16), (4, 4))
    term = after(term, near_1)
    (term,) = on_chip(repack_kernel, [(term.shape, BF16)])(term, move(term, (1, 2)))
    term = after(term, far_2, near_2)
    (term,) = on_chip(unpack_kernel, [((share + 8, width_out), F32)])(term, move(term, (2, 1)))
    near_parts = near_parts + (from_8, from_12, from_4)
    grad_features = plus(*((part, 0, one) for part in near_parts)).astype(BF16)

    grad_weight, grad_bias = on_chip(
        partial(final_kernel, scale=scale_factor),
        [((width_in, width_out), F32), ((1, width_out), F32)],
        (),
        1,
    )(rep, term, swap_rep(term, 1, 2))
    return (output, grad_features, grad_weight, grad_bias.reshape(width_out))


def general_body(node_features, weight, bias_vector, tile_values, tile_place, tile_count, cotangent):
    loop_size = lax.axis_size("loop")
    rep_size = lax.axis_size("rep")
    position = lax.axis_index("loop").astype(jnp.int32)
    rep = lax.axis_index("rep").astype(jnp.int32)
    rows_own, width_in = node_features.shape
    width_out = weight.shape[1]
    partners, tile = tile_values.shape[2], tile_values.shape[4]
    per_side = rows_own // tile
    panel = rep_size * per_side
    order = axis_order(loop_size)
    half = partners // 2
    share = width_in // rep_size
    scale_factor = float(rows_own * loop_size * rep_size) ** (-0.5)
    tiles = tile_values[0, 0]
    rep_bits = [1 << bit for bit in range(rep_size.bit_length() - 1)]
    partner = jnp.bitwise_xor(position, jnp.array(partner_masks(order), jnp.int32))
    target, source = slot_targets(tile_place, tile_count, partner, rep, per_side)

    def move(value, bit):
        return exchange(value, (bit, bit), loop_size, rep_size)

    gathered = node_features
    for bit in order:
        gathered = jnp.concatenate([gathered, move(gathered, bit)], axis=0)
    cotangent_rows = cotangent
    for bit in rep_bits:
        cotangent_rows = jnp.concatenate(
            [cotangent_rows, swap_rep(cotangent_rows, bit, rep_size)], axis=0
        )
    sums = tile_loop(
        target, source, partner, tiles, jnp.zeros((panel * tile, width_in), F32),
        lambda k, s: lax.dynamic_slice_in_dim(
            gathered, k * rows_own + source[k, s] * tile, tile, 0
        ),
        dot,
        lambda k, s: jnp.maximum(target[k, s], 0) * tile,
    )
    for bit in rep_bits:
        other = swap_rep(sums, bit, rep_size)
        blocks = other.reshape(rep_size, rows_own, width_in)
        blocks = jnp.stack([blocks[t ^ bit] for t in range(rep_size)])
        sums = sums + blocks.reshape(sums.shape)
    high = lax.reduce_precision(sums, 8, 7)
    low = (sums - high).astype(BF16)
    high = high.astype(BF16)
    preact = dot(high, weight) + dot(low, weight) + bias_vector[None, :]
    negative = jnp.minimum(preact, 0.0)
    own = preact[:rows_own]
    output = jnp.where(own > 0, own, jnp.expm1(negative[:rows_own])).astype(BF16)
    slope = jnp.where(preact > 0, 1.0, jnp.exp(negative))
    grad_pre = (cotangent_rows.astype(F32) * slope).astype(BF16)
    back = dot(grad_pre, weight, ((1,), (1,))).astype(BF16)
    start = rep * share
    term = dot(lax.dynamic_slice_in_dim(high, start, share, 1), grad_pre, ((0,), (0,)))
    term = term + dot(lax.dynamic_slice_in_dim(low, start, share, 1), grad_pre, ((0,), (0,)))
    bias_term = jnp.sum(grad_pre[:rows_own].astype(F32), axis=0, keepdims=True)
    term = jnp.concatenate([term, jnp.broadcast_to(bias_term, (8, width_out))], axis=0)
    adjoint = tile_loop(
        target, source, partner, tiles, jnp.zeros((partners * rows_own, width_in), F32),
        lambda k, s: lax.dynamic_slice_in_dim(back, jnp.maximum(target[k, s], 0) * tile, tile, 0),
        lambda left, right: dot(left, right, ((0,), (0,))),
        lambda k, s: k * rows_own + source[k, s] * tile,
    )
    size = half * rows_own
    for bit in order[::-1]:
        term = term + move(term, bit)
        adjoint = adjoint[:size] + move(adjoint[size:].astype(BF16), bit).astype(F32)
        size = size // 2
    shares = term[None] * scale_factor
    for bit in rep_bits:
        shares = jnp.concatenate([shares, swap_rep(shares, bit, rep_size)], axis=0)
    shares = shares[jnp.bitwise_xor(jnp.arange(rep_size, dtype=jnp.int32), rep)]
    grad_weight = shares[:, :share].reshape(width_in, width_out)
    return (output, adjoint.astype(BF16), grad_weight, jnp.sum(shares[:, share], axis=0))


def body(*arrays):
    rows_own, tile_values = arrays[0].shape[0], arrays[3]
    _, _, partners, slots, tile, _ = tile_values.shape
    groups = (lax.axis_size("rep"), partners, slots, rows_own // tile)
    return (dense_body if groups == (2, 16, 2, 1) else general_body)(*arrays)


def solution(mesh):
    return jax.shard_map(
        body,
        mesh=mesh,
        in_specs=(
            P(("loop", "rep"), None),
            P(),
            P(),
            P("loop", "rep", None, None, None, None),
            P("loop", "rep", None, None),
            P("loop", "rep", None),
            P(("loop", "rep"), None),
        ),
        out_specs=(P(("loop", "rep"), None), P(("loop", "rep"), None), P(), P()),
        check_vma=False,
    )
```
